256 devices in a mesh: section: 8 (over y, core), ctx: 32 (over z, x).
Axes of the slice: x: 4, y: 4, z: 8, core: 2. Of those that a mesh axis runs over, the one named last changes fastest.
Arguments:
- features: bfloat16 [8, 8192, 1536], P('section', 'ctx'), may hold values from -6 to 6
- conv_weight: float32 [8, 3, 1536], P('section'), may hold values from -3.5 to 3.5
- residues: float32 [8, 32, 16], P('section'), may hold values from -1.5 to 1.5
- decay_rates: float32 [8, 32, 16], P('section'), may hold values from 6.1035156e-05 to 0.1
- skip_gain: float32 [8, 512], P('section'), may hold values from -6 to 6
Outputs:
- passed: bfloat16 [8, 8192, 512], P('section', 'ctx')
The draws below stay inside these ranges and needn't reach their ends.
All inputs are finite; a program needn't handle non-finite values.
Results may differ from the reference program's by a relative error of at most 0.0014.
Values may be sent and summed in bfloat16 or wider, within the bound.
A program may use at most 64 MiB of HBM per device.

```python
import math
import jax
import jax.numpy as jnp
from jax import lax

C = 512
G = 32
MODES = 16
KS = 3
L = 8192
N_SECTION = 8


def block_levels(rng, dims, pieces, low, high):
    level = 1.0
    for position, shards_of in pieces:
        steps = jax.random.uniform(jax.random.fold_in(jax.random.fold_in(rng, 6), position), (shards_of,), jnp.float32, low / len(pieces), high / len(pieces))
        level = level * jnp.repeat(jnp.exp(steps), dims[position] // shards_of).reshape((-1,) + (1,) * (len(dims) - 1 - position))
    return level


def scatter_about(rng, dims, deviation, bound, split=(), dtype=jnp.bfloat16):
    factor_of = block_levels(rng, dims, split, -0.22, 0.18) if split else 1.0
    entries = jax.random.normal(rng, dims, jnp.float32) * deviation * factor_of
    return jnp.minimum(jnp.maximum(entries, -bound), bound).astype(dtype)


def setup_inputs(seed: int = 0) -> dict:
    key_of = jax.random.split(jax.random.key(seed), 6)
    features = scatter_about(key_of[0], (N_SECTION, L, 3 * C), 1.0, 6.0, ((0, 8), (1, 32)))
    conv_weight = scatter_about(key_of[1], (N_SECTION, KS, 3 * C), 0.6, 3.5, ((0, 8),), jnp.float32)
    residues = scatter_about(key_of[2], (N_SECTION, G, MODES), 0.25, 1.5, ((0, 8),), jnp.float32)
    decay_rates = jnp.clip(jnp.exp(math.log(0.1) - 7.4014754 * jax.random.uniform(key_of[3], (N_SECTION, G, MODES), jnp.float32) ** block_levels(key_of[3], (N_SECTION, G, MODES), ((0, 8),), -0.2, 0.2)), 6.103515625e-05, 0.1)
    skip_gain = scatter_about(key_of[4], (N_SECTION, C), 1.0, 6.0, ((0, 8),), jnp.float32)
    return dict(features=features, conv_weight=conv_weight, residues=residues, decay_rates=decay_rates, skip_gain=skip_gain)


HIGHEST = lax.Precision.HIGHEST

def section_mixer(features, conv_weight, residues, decay_rates, skip_gain):
    seq_rows = features.shape[0]
    values = features.astype(jnp.float32)
    padded = jnp.concatenate([jnp.zeros((KS - 1, values.shape[1]), jnp.float32), values], axis=0)
    shortened = jnp.zeros(values.shape, jnp.float32)
    for tap_index in range(KS):
        begin_row = KS - 1 - tap_index
        shortened = shortened + conv_weight[tap_index][None, :] * padded[begin_row:begin_row + seq_rows]
    query_part = shortened[:, :C]
    key_part = shortened[:, C:2 * C]
    value_part = shortened[:, 2 * C:]
    gated_input = key_part * value_part
    time_index = jnp.arange(seq_rows).astype(jnp.float32)
    scaled = residues * jnp.sqrt(-jnp.expm1(-2.0 * decay_rates))
    envelope = jnp.exp(-decay_rates[None, :, :] * time_index[:, None, None])
    filter_time = jnp.einsum('gm,tgm->tg', scaled, envelope, precision=HIGHEST)
    gated_spec = jnp.fft.rfft(gated_input, n=2 * seq_rows, axis=0)
    filter_spec = jnp.repeat(jnp.fft.rfft(filter_time, n=2 * seq_rows, axis=0), C // G, axis=1)
    convolved = jnp.fft.irfft(gated_spec * filter_spec, n=2 * seq_rows, axis=0)[:seq_rows]
    mixer_sum = convolved + skip_gain[None, :] * gated_input
    return (query_part * mixer_sum).astype(jnp.bfloat16)

def reference(features, conv_weight, residues, decay_rates, skip_gain):
    results = []
    for section_number in range(N_SECTION):
        results.append(section_mixer(features[section_number], conv_weight[section_number], residues[section_number], decay_rates[section_number], skip_gain[section_number]))
    return jnp.roll(jnp.stack(results, axis=0), 1, axis=0)
```

```python
import functools

import jax
import jax.numpy as jnp
from jax import lax
from jax.experimental import pallas as pl
from jax.experimental.pallas import tpu as pltpu
from jax.sharding import PartitionSpec as P

MESH = pl.DeviceIdType.MESH
HIGHEST = lax.Precision.HIGHEST
F32 = jnp.float32
BF16 = jnp.bfloat16
NX = 4
LANES = 128
STEP = 8


def iota(shape, axis):
    return lax.broadcasted_iota(jnp.int32, shape, axis)


def split(value):
    high = value.astype(BF16)
    return high, (value - high.astype(F32)).astype(BF16)


def dot3(left, right):
    dot = functools.partial(jnp.dot, preferred_element_type=F32)
    return dot(left[0], right[0]) + (dot(left[1], right[0]) + dot(left[0], right[1]))


def mode_scale(residues, decay):
    twice = 2.0 * decay
    series = jnp.full_like(twice, 1.0)
    for order in range(10, 1, -1):
        series = 1.0 - series * twice * (1.0 / order)
    gain = jnp.where(twice < 0.5, twice * series, 1.0 - jnp.exp(-twice))
    return residues * jnp.sqrt(gain)


def over_channels(table, channels):
    groups = table.shape[1]
    pick = (iota((groups, channels), 0) == iota((groups, channels), 1) // (channels // groups)).astype(F32)
    return lax.dot_general(table, pick, (((1,), (0,)), ((), ())), precision=HIGHEST, preferred_element_type=F32)


def flat_row(table):
    modes, groups = table.shape
    size = groups * modes
    pick = (iota((modes, size), 0) == iota((modes, size), 1) % modes).astype(F32)
    spread = lax.dot_general(table, pick, (((0,), (0,)), ((), ())), precision=HIGHEST, preferred_element_type=F32)
    keep = iota((groups, size), 0) == iota((groups, size), 1) // modes
    return jnp.sum(jnp.where(keep, spread, 0.0), axis=0, keepdims=True)


def kernel(
    n_section, n_ctx, rows, channels, groups, modes,
    feat_ref, conv_ref, res_ref, dec_ref, skip_ref, out_ref,
    kv, qlast, own_lam, own_w, gate_hi, gate_lo, outbox, esend, p1, ebox, rsend, p2, acc, pre, hsend, p3,
    fbox, halo, conv_in, res_in, dec_in, skip_in, gated, query, mixed, out_hi, out_lo,
    local_sem, par_send, par_recv, feat_send, feat_recv, halo_send, halo_recv,
    p1_send, p1_recv, edge_send, edge_recv, p2_send, p2_recv, p3_send, p3_recv,
):
    nz = n_ctx // NX
    tiles = channels // LANES
    per = channels // groups
    block = (LANES // per) * modes
    sec = lax.axis_index("section")
    ctx = lax.axis_index("ctx")
    z = ctx // NX
    x = ctx % NX
    sec_next = (sec + 1) % n_section
    sec_prev = (sec + n_section - 1) % n_section

    kv_copy = pltpu.make_async_copy(feat_ref.at[0, :, pl.ds(channels, 2 * channels)], kv, local_sem.at[0])
    kv_copy.start()
    q_copy = pltpu.make_async_copy(feat_ref.at[0, pl.ds(rows - 16, 16), pl.ds(0, channels)], qlast, local_sem.at[1])
    q_copy.start()

    barrier = pltpu.get_barrier_semaphore()

    def greet(section, position):
        pl.semaphore_signal(barrier, inc=1, device_id=(section, position), device_id_type=MESH)

    z_next = (z + 1) % nz
    z_prev = (z + nz - 1) % nz
    for o in range(1, nz):
        greet(sec, ((z + o) % nz) * NX + x)
    for o in range(1, NX):
        greet(sec, z * NX + (x + o) % NX)
        greet(sec, z_next * NX + (x + o) % NX)
        greet(sec, z_prev * NX + (x + o) % NX)
    for o in range(NX):
        greet(sec_next, z * NX + o)
        greet(sec_prev, z * NX + o)

    @pl.when(x == NX - 1)
    def _():
        greet(sec_next, z_next * NX)

    @pl.when(x == 0)
    def _():
        greet(sec_prev, z_prev * NX + NX - 1)

    n_greet = (nz - 1) + 3 * (NX - 1) + 2 * NX

    decay = dec_ref[0]
    scale = mode_scale(res_ref[0], decay)
    lam_wide = over_channels(decay, channels)
    w_wide = over_channels(scale, channels)
    lam_row = flat_row(decay)
    w_row = flat_row(scale)
    for j in range(tiles):
        own_lam[j] = lam_wide[:, j * LANES:(j + 1) * LANES]
        own_w[j] = w_wide[:, j * LANES:(j + 1) * LANES]

    kv_copy.wait()
    q_copy.wait()
    row = iota((rows, LANES), 0)
    to_end = (rows - 1 - row).astype(F32)
    keep = iota((block, LANES), 0) // modes == iota((block, LANES), 1) // per

    for j in range(tiles):
        parts = []
        edges = []
        for part in range(2):
            cols = pl.ds(part * channels + j * LANES, LANES)
            value = kv[:, cols].astype(F32)
            taps = [conv_ref[i, :, pl.ds((part + 1) * channels + j * LANES, LANES)] for i in range(3)]
            parts.append(taps[0] * value + taps[1] * pltpu.roll(value, 1, 0) + taps[2] * pltpu.roll(value, 2, 0))
            edges.append(value)
            esend[:, pl.ds((part + 1) * channels + j * LANES, LANES)] = value[rows - 2:]
        esend[:, pl.ds(j * LANES, LANES)] = qlast[:, pl.ds(j * LANES, LANES)].astype(F32)[14:]
        gate = split(jnp.where(row >= 2, parts[0] * parts[1], 0.0))
        rising = w_row[:, j * block:(j + 1) * block] * jnp.exp(-lam_row[:, j * block:(j + 1) * block] * to_end)
        state = dot3(split(rising.T), gate)
        state = jnp.where(keep, state, 0.0).reshape(block // modes, modes, LANES).sum(axis=0)
        outbox[j, pl.ds(0, modes)] = state
        outbox[j, pl.ds(modes, 8)] = jnp.concatenate(
            [edges[0][rows - 2:], edges[1][rows - 2:], edges[0][:2], edges[1][:2]], axis=0
        )

    pl.semaphore_wait(barrier, n_greet + (x == NX - 1).astype(jnp.int32) + (x == 0).astype(jnp.int32))

    def send(source, target, send_sem, recv_sem, section, position):
        return pltpu.make_async_remote_copy(
            src_ref=source, dst_ref=target, send_sem=send_sem, recv_sem=recv_sem,
            device_id=(section, position), device_id_type=MESH,
        )

    p1_copies = []
    for o in range(1, NX):
        q = (x + o) % NX
        p1_copies.append(send(outbox.at[q], p1.at[o], p1_send.at[o], p1_recv.at[o], sec, z * NX + q))
        p1_copies[-1].start()

    def edge_copy(q):
        return send(
            outbox.at[q, pl.ds(modes, 8)], ebox, edge_send.at[q], edge_recv.at[0], sec,
            (z + 1) % nz * NX + q,
        )

    @pl.when(jnp.logical_and(x == NX - 1, z < nz - 1))
    def _():
        for q in range(NX):
            edge_copy(q).start()

    ship = []
    for n, (source, target) in enumerate(((conv_ref, conv_in), (res_ref, res_in), (dec_ref, dec_in), (skip_ref, skip_in))):
        ship.append(send(source, target, par_send.at[n], par_recv.at[n], sec_next, ctx))
    feat_copies = []
    for j in range(tiles):
        for part in range(3):
            feat_copies.append(
                send(
                    feat_ref.at[0, :, pl.ds(part * channels + j * LANES, LANES)], fbox.at[j, part],
                    feat_send.at[j, part], feat_recv.at[j, part], sec_next, ctx,
                )
            )
    halo_copy = send(esend, halo, halo_send.at[0], halo_recv.at[0], sec_next, (ctx + 1) % n_ctx)
    for copy in ship + [halo_copy] + feat_copies:
        copy.start()

    p1[0] = outbox[x]

    @pl.when(z == 0)
    def _():
        ebox[...] = jnp.zeros_like(ebox)

    acc[...] = jnp.zeros_like(acc)
    lam = own_lam[x]
    w_own = own_w[x]
    for copy in p1_copies:
        copy.wait_recv()

    @pl.when(z > 0)
    def _():
        edge_copy(0).wait_recv()

    span = float(rows)
    fade_row = jnp.exp(-span * lam)
    first = w_own * jnp.exp(-(span - 1.0) * lam)
    second = w_own * jnp.exp(-(span - 2.0) * lam)
    taps = [
        [conv_ref[i, :, pl.ds(pl.multiple_of((part + 1) * channels + x * LANES, LANES), LANES)] for i in range(3)]
        for part in range(2)
    ]
    before = ebox[...]
    total = jnp.zeros((modes, LANES), F32)
    for member in range(NX):
        slot = (x + NX - member) % NX
        edge = p1[slot, pl.ds(modes, 8)]
        products = []
        for part in range(2):
            old2 = before[2 * part:2 * part + 1]
            old1 = before[2 * part + 1:2 * part + 2]
            new0 = edge[4 + 2 * part:5 + 2 * part]
            new1 = edge[5 + 2 * part:6 + 2 * part]
            t0, t1, t2 = taps[part]
            products.append((t0 * new0 + t1 * old1 + t2 * old2, t0 * new1 + t1 * new0 + t2 * old1))
        state = p1[slot, pl.ds(0, modes)]
        state = state + first * (products[0][0] * products[1][0]) + second * (products[0][1] * products[1][1])
        pre[member] = total
        total = fade_row * total + state
        before = edge
    rsend[...] = total

    def p2_copy(o):
        return send(rsend, p2.at[o], p2_send.at[o], p2_recv.at[o], sec, (z + o) % nz * NX + x)

    order = sorted(range(1, nz), key=lambda o: (-min(o, nz - o), o))
    for o in order:
        @pl.when(z + o < nz)
        def _(o=o):
            p2_copy(o).start()

    for copy in ship:
        copy.wait_recv()
    halo_copy.wait_recv()

    @pl.when(ctx == 0)
    def _():
        halo[...] = jnp.zeros_like(halo)

    decay_in = dec_in[0]
    scale_in = mode_scale(res_in[0], decay_in)
    lam_in = over_channels(decay_in, channels)
    w_in = over_channels(scale_in, channels)
    row_in = flat_row(decay_in)
    for j in range(tiles):
        falling = jnp.exp(-row_in[:, j * block:(j + 1) * block] * (row + 1).astype(F32))
        high, low = split(falling)
        out_hi[:, pl.ds(j * block, block)] = high
        out_lo[:, pl.ds(j * block, block)] = low

    def local_tile(j):
        cols = pl.ds(j * LANES, LANES)
        for part in range(3):
            feat_copies[3 * j + part].wait_recv()
        shaped = []
        for part in range(3):
            value = fbox[j, part].astype(F32)
            wide = pl.ds(part * channels + j * LANES, LANES)
            edge = halo[:, wide]
            one = jnp.where(row == 0, edge[1:2], pltpu.roll(value, 1, 0))
            two = jnp.where(row == 0, edge[0:1], jnp.where(row == 1, edge[1:2], pltpu.roll(value, 2, 0)))
            t0, t1, t2 = [conv_in[i, :, wide] for i in range(3)]
            shaped.append(t0 * value + t1 * one + t2 * two)
        query[:, cols] = shaped[0]
        gated[:, cols] = shaped[1] * shaped[2]
        lam_j = lam_in[:, j * LANES:(j + 1) * LANES]
        w_j = w_in[:, j * LANES:(j + 1) * LANES]
        gain = skip_in[:, cols]
        step_row = iota((STEP, LANES), 0)
        near = []
        enter = []
        for i in range(STEP):
            faded = w_j * jnp.exp(-float(i) * lam_j)
            tap = jnp.sum(faded, axis=0, keepdims=True)
            near.append(jnp.where(step_row >= i, tap, 0.0))
            enter.append(faded)
        near[0] = near[0] + gain
        ahead = (step_row + 1).astype(F32)
        leave = [jnp.exp(-lam_j[m:m + 1] * ahead) for m in range(modes)]
        fade = jnp.exp(-float(STEP) * lam_j)

        def body(k, state):
            at = pl.ds(pl.multiple_of(k * STEP, STEP), STEP)
            now = gated[at, cols]
            value = near[0] * now
            for i in range(1, STEP):
                value = value + near[i] * pltpu.roll(now, i, 0)
            for m in range(modes):
                value = value + leave[m] * state[m:m + 1]
            mixed[at, cols] = value
            state = fade * state
            for i in range(STEP):
                state = state + enter[STEP - 1 - i] * now[i:i + 1]
            return state

        lax.fori_loop(0, rows // STEP, body, jnp.zeros((modes, LANES), F32))

    for j in range(tiles // 2):
        local_tile(j)

    fade_z = jnp.exp(-(span * NX) * lam)
    for o in range(nz - 1, 0, -1):
        @pl.when(z >= o)
        def _(o=o):
            p2_copy(o).wait_recv()
            acc[...] = fade_z * acc[...] + p2[o]

    carry = acc[...]
    p3_copies = []
    for member in range(NX):
        hsend[member] = carry + pre[member]
        carry = fade_row * carry
        p3_copies.append(
            send(hsend.at[member], p3.at[x], p3_send.at[member], p3_recv.at[x], sec_next, z * NX + member)
        )
        p3_copies[-1].start()

    for j in range(tiles // 2, tiles):
        local_tile(j)

    for j in range(tiles):
        cols = pl.ds(j * LANES, LANES)
        send(hsend.at[0], p3.at[j], p3_send.at[0], p3_recv.at[j], sec_next, ctx).wait_recv()
        state = p3[j]
        spread = jnp.where(keep, jnp.concatenate([state] * (block // modes), axis=0), 0.0)
        wide = pl.ds(j * block, block)
        carried = dot3((out_hi[:, wide], out_lo[:, wide]), split(spread))
        out_ref[0, :, cols] = (query[:, cols] * (mixed[:, cols] + carried)).astype(BF16)

    for copy in ship + [halo_copy] + feat_copies + p1_copies + p3_copies:
        copy.wait_send()

    @pl.when(jnp.logical_and(x == NX - 1, z < nz - 1))
    def _():
        for q in range(NX):
            edge_copy(q).wait_send()

    for o in range(1, nz):
        @pl.when(z + o < nz)
        def _(o=o):
            p2_copy(o).wait_send()


def on_device(n_section, n_ctx, features, conv_weight, residues, decay_rates, skip_gain):
    _, rows, width = features.shape
    channels = skip_gain.shape[1]
    _, groups, modes = residues.shape
    tiles = channels // LANES
    nz = n_ctx // NX
    vmem = pltpu.VMEM
    dma = pltpu.SemaphoreType.DMA
    whole = pl.BlockSpec(memory_space=pltpu.VMEM)
    conv_weight = jnp.swapaxes(conv_weight, 0, 1)
    residues = jnp.swapaxes(residues, 1, 2)
    decay_rates = jnp.swapaxes(decay_rates, 1, 2)
    return pl.pallas_call(
        functools.partial(kernel, n_section, n_ctx, rows, channels, groups, modes),
        out_shape=jax.ShapeDtypeStruct((1, rows, channels), BF16),
        in_specs=[pl.BlockSpec(memory_space=pl.ANY)] + [whole] * 4,
        out_specs=whole,
        scratch_shapes=[
            vmem((rows, 2 * channels), BF16),
            vmem((16, channels), BF16),
            vmem((tiles, modes, LANES), F32),
            vmem((tiles, modes, LANES), F32),
            vmem((rows, LANES), BF16),
            vmem((rows, LANES), BF16),
            vmem((tiles, modes + 8, LANES), F32),
            vmem((2, width), F32),
            vmem((NX, modes + 8, LANES), F32),
            vmem((8, LANES), F32),
            vmem((modes, LANES), F32),
            vmem((nz, modes, LANES), F32),
            vmem((modes, LANES), F32),
            vmem((NX, modes, LANES), F32),
            vmem((NX, modes, LANES), F32),
            vmem((tiles, modes, LANES), F32),
            vmem((tiles, 3, rows, LANES), BF16),
            vmem((2, width), F32),
            vmem(conv_weight.shape, F32),
            vmem(residues.shape, F32),
            vmem(decay_rates.shape, F32),
            vmem(skip_gain.shape, F32),
            vmem((rows, channels), F32),
            vmem((rows, channels), F32),
            vmem((rows, channels), F32),
            vmem((rows, groups * modes), BF16),
            vmem((rows, groups * modes), BF16),
            dma((2,)),
            dma((4,)), dma((4,)),
            dma((tiles, 3)), dma((tiles, 3)),
            dma((1,)), dma((1,)),
            dma((NX,)), dma((NX,)),
            dma((NX,)), dma((1,)),
            dma((nz,)), dma((nz,)),
            dma((NX,)), dma((NX,)),
        ],
        compiler_params=pltpu.CompilerParams(collective_id=0, has_side_effects=True),
        name="mixer",
    )(features, conv_weight, residues, decay_rates, skip_gain)


def solution(mesh):
    placed = (
        P("section", "ctx", None),
        P("section", None, None),
        P("section", None, None),
        P("section", None, None),
        P("section", None),
    )
    body = functools.partial(on_device, mesh.shape["section"], mesh.shape["ctx"])
    return jax.shard_map(body, mesh=mesh, in_specs=placed, out_specs=P("section", "ctx", None), check_vma=False)
```

```python
import functools

import jax
import jax.numpy as jnp
from jax import lax
from jax.experimental import pallas as pl
from jax.experimental.pallas import tpu as pltpu
from jax.sharding import PartitionSpec as P

MESH = pl.DeviceIdType.MESH
HIGHEST = lax.Precision.HIGHEST
F32 = jnp.float32
BF16 = jnp.bfloat16
NX = 4
LANES = 128
CHUNKS = 8


def iota(shape, axis):
    return lax.broadcasted_iota(jnp.int32, shape, axis)


def split(value):
    high = value.astype(BF16)
    return high, (value - high.astype(F32)).astype(BF16)


def dot3(left, right):
    dot = functools.partial(jnp.dot, preferred_element_type=F32)
    return dot(left[0], right[0]) + (dot(left[1], right[0]) + dot(left[0], right[1]))


def mode_scale(residues, decay):
    twice = 2.0 * decay
    series = jnp.full_like(twice, 1.0)
    for order in range(10, 1, -1):
        series = 1.0 - series * twice * (1.0 / order)
    gain = jnp.where(twice < 0.5, twice * series, 1.0 - jnp.exp(-twice))
    return residues * jnp.sqrt(gain)


def over_channels(table, channels):
    groups = table.shape[1]
    pick = (iota((groups, channels), 0) == iota((groups, channels), 1) // (channels // groups)).astype(F32)
    return lax.dot_general(table, pick, (((1,), (0,)), ((), ())), precision=HIGHEST, preferred_element_type=F32)


def flat_row(table):
    modes, groups = table.shape
    size = groups * modes
    pick = (iota((modes, size), 0) == iota((modes, size), 1) % modes).astype(F32)
    spread = lax.dot_general(table, pick, (((0,), (0,)), ((), ())), precision=HIGHEST, preferred_element_type=F32)
    keep = iota((groups, size), 0) == iota((groups, size), 1) // modes
    return jnp.sum(jnp.where(keep, spread, 0.0), axis=0, keepdims=True)


def kernel(
    n_section, n_ctx, rows, channels, groups, modes,
    feat_ref, conv_ref, res_ref, dec_ref, skip_ref, out_ref,
    kv, qlast, own_lam, own_w, gate_hi, gate_lo, outbox, esend, p1, ebox, rsend, p2, acc, pre, hsend, p3,
    fbox, halo, conv_in, res_in, dec_in, skip_in, gated, query, mixed, out_hi, out_lo,
    local_sem, par_send, par_recv, feat_send, feat_recv, halo_send, halo_recv,
    p1_send, p1_recv, edge_send, edge_recv, p2_send, p2_recv, p3_send, p3_recv,
):
    nz = n_ctx // NX
    tiles = channels // LANES
    length = rows // CHUNKS
    per = channels // groups
    block = (LANES // per) * modes
    sec = lax.axis_index("section")
    ctx = lax.axis_index("ctx")
    z = ctx // NX
    x = ctx % NX
    sec_next = (sec + 1) % n_section
    sec_prev = (sec + n_section - 1) % n_section

    kv_copy = pltpu.make_async_copy(feat_ref.at[0, :, pl.ds(channels, 2 * channels)], kv, local_sem.at[0])
    kv_copy.start()
    q_copy = pltpu.make_async_copy(feat_ref.at[0, pl.ds(rows - 16, 16), pl.ds(0, channels)], qlast, local_sem.at[1])
    q_copy.start()

    barrier = pltpu.get_barrier_semaphore()

    def greet(section, position):
        pl.semaphore_signal(barrier, inc=1, device_id=(section, position), device_id_type=MESH)

    z_next = (z + 1) % nz
    z_prev = (z + nz - 1) % nz
    for o in range(1, nz):
        greet(sec, ((z + o) % nz) * NX + x)
    for o in range(1, NX):
        greet(sec, z * NX + (x + o) % NX)
        greet(sec, z_next * NX + (x + o) % NX)
        greet(sec, z_prev * NX + (x + o) % NX)
    for o in range(NX):
        greet(sec_next, z * NX + o)
        greet(sec_prev, z * NX + o)

    @pl.when(x == NX - 1)
    def _():
        greet(sec_next, z_next * NX)

    @pl.when(x == 0)
    def _():
        greet(sec_prev, z_prev * NX + NX - 1)

    n_greet = (nz - 1) + 3 * (NX - 1) + 2 * NX

    decay = dec_ref[0]
    scale = mode_scale(res_ref[0], decay)
    lam_wide = over_channels(decay, channels)
    w_wide = over_channels(scale, channels)
    lam_row = flat_row(decay)
    w_row = flat_row(scale)
    for j in range(tiles):
        own_lam[j] = lam_wide[:, j * LANES:(j + 1) * LANES]
        own_w[j] = w_wide[:, j * LANES:(j + 1) * LANES]

    kv_copy.wait()
    q_copy.wait()
    row = iota((rows, LANES), 0)
    to_end = (rows - 1 - row).astype(F32)
    keep = iota((block, LANES), 0) // modes == iota((block, LANES), 1) // per

    for j in range(tiles):
        parts = []
        edges = []
        for part in range(2):
            cols = pl.ds(part * channels + j * LANES, LANES)
            value = kv[:, cols].astype(F32)
            taps = [conv_ref[i, :, pl.ds((part + 1) * channels + j * LANES, LANES)] for i in range(3)]
            parts.append(taps[0] * value + taps[1] * pltpu.roll(value, 1, 0) + taps[2] * pltpu.roll(value, 2, 0))
            edges.append(value)
            esend[:, pl.ds((part + 1) * channels + j * LANES, LANES)] = value[rows - 2:]
        esend[:, pl.ds(j * LANES, LANES)] = qlast[:, pl.ds(j * LANES, LANES)].astype(F32)[14:]
        gate = split(jnp.where(row >= 2, parts[0] * parts[1], 0.0))
        rising = w_row[:, j * block:(j + 1) * block] * jnp.exp(-lam_row[:, j * block:(j + 1) * block] * to_end)
        state = dot3(split(rising.T), gate)
        state = jnp.where(keep, state, 0.0).reshape(block // modes, modes, LANES).sum(axis=0)
        outbox[j, pl.ds(0, modes)] = state
        outbox[j, pl.ds(modes, 8)] = jnp.concatenate(
            [edges[0][rows - 2:], edges[1][rows - 2:], edges[0][:2], edges[1][:2]], axis=0
        )

    pl.semaphore_wait(barrier, n_greet + (x == NX - 1).astype(jnp.int32) + (x == 0).astype(jnp.int32))

    def send(source, target, send_sem, recv_sem, section, position):
        return pltpu.make_async_remote_copy(
            src_ref=source, dst_ref=target, send_sem=send_sem, recv_sem=recv_sem,
            device_id=(section, position), device_id_type=MESH,
        )

    p1_copies = []
    for o in range(1, NX):
        q = (x + o) % NX
        p1_copies.append(send(outbox.at[q], p1.at[o], p1_send.at[o], p1_recv.at[o], sec, z * NX + q))
        p1_copies[-1].start()

    def edge_copy(q):
        return send(
            outbox.at[q, pl.ds(modes, 8)], ebox, edge_send.at[q], edge_recv.at[0], sec,
            (z + 1) % nz * NX + q,
        )

    @pl.when(jnp.logical_and(x == NX - 1, z < nz - 1))
    def _():
        for q in range(NX):
            edge_copy(q).start()

    ship = []
    for n, (source, target) in enumerate(((conv_ref, conv_in), (res_ref, res_in), (dec_ref, dec_in), (skip_ref, skip_in))):
        ship.append(send(source, target, par_send.at[n], par_recv.at[n], sec_next, ctx))
    feat_copies = []
    for j in range(tiles):
        for part in range(3):
            feat_copies.append(
                send(
                    feat_ref.at[0, :, pl.ds(part * channels + j * LANES, LANES)], fbox.at[j, part],
                    feat_send.at[j, part], feat_recv.at[j, part], sec_next, ctx,
                )
            )
    halo_copy = send(esend, halo, halo_send.at[0], halo_recv.at[0], sec_next, (ctx + 1) % n_ctx)
    for copy in ship + [halo_copy] + feat_copies:
        copy.start()

    p1[0] = outbox[x]

    @pl.when(z == 0)
    def _():
        ebox[...] = jnp.zeros_like(ebox)

    acc[...] = jnp.zeros_like(acc)
    lam = own_lam[x]
    w_own = own_w[x]
    for copy in p1_copies:
        copy.wait_recv()

    @pl.when(z > 0)
    def _():
        edge_copy(0).wait_recv()

    span = float(rows)
    fade_row = jnp.exp(-span * lam)
    first = w_own * jnp.exp(-(span - 1.0) * lam)
    second = w_own * jnp.exp(-(span - 2.0) * lam)
    taps = [
        [conv_ref[i, :, pl.ds(pl.multiple_of((part + 1) * channels + x * LANES, LANES), LANES)] for i in range(3)]
        for part in range(2)
    ]
    before = ebox[...]
    total = jnp.zeros((modes, LANES), F32)
    for member in range(NX):
        slot = (x + NX - member) % NX
        edge = p1[slot, pl.ds(modes, 8)]
        products = []
        for part in range(2):
            old2 = before[2 * part:2 * part + 1]
            old1 = before[2 * part + 1:2 * part + 2]
            new0 = edge[4 + 2 * part:5 + 2 * part]
            new1 = edge[5 + 2 * part:6 + 2 * part]
            t0, t1, t2 = taps[part]
            products.append((t0 * new0 + t1 * old1 + t2 * old2, t0 * new1 + t1 * new0 + t2 * old1))
        state = p1[slot, pl.ds(0, modes)]
        state = state + first * (products[0][0] * products[1][0]) + second * (products[0][1] * products[1][1])
        pre[member] = total
        total = fade_row * total + state
        before = edge
    rsend[...] = total

    def p2_copy(o):
        return send(rsend, p2.at[o], p2_send.at[o], p2_recv.at[o], sec, (z + o) % nz * NX + x)

    order = sorted(range(1, nz), key=lambda o: (-min(o, nz - o), o))
    for o in order:
        @pl.when(z + o < nz)
        def _(o=o):
            p2_copy(o).start()

    for copy in ship:
        copy.wait_recv()
    halo_copy.wait_recv()

    @pl.when(ctx == 0)
    def _():
        halo[...] = jnp.zeros_like(halo)

    decay_in = dec_in[0]
    scale_in = mode_scale(res_in[0], decay_in)
    lam_in = over_channels(decay_in, channels)
    w_in = over_channels(scale_in, channels)
    row_in = flat_row(decay_in)
    for j in range(tiles):
        falling = jnp.exp(-row_in[:, j * block:(j + 1) * block] * (row + 1).astype(F32))
        high, low = split(falling)
        out_hi[:, pl.ds(j * block, block)] = high
        out_lo[:, pl.ds(j * block, block)] = low

    def local_tile(j):
        cols = pl.ds(j * LANES, LANES)
        for part in range(3):
            feat_copies[3 * j + part].wait_recv()
        shaped = []
        for part in range(3):
            value = fbox[j, part].astype(F32)
            wide = pl.ds(part * channels + j * LANES, LANES)
            edge = halo[:, wide]
            one = jnp.where(row == 0, edge[1:2], pltpu.roll(value, 1, 0))
            two = jnp.where(row == 0, edge[0:1], jnp.where(row == 1, edge[1:2], pltpu.roll(value, 2, 0)))
            t0, t1, t2 = [conv_in[i, :, wide] for i in range(3)]
            shaped.append(t0 * value + t1 * one + t2 * two)
        query[:, cols] = shaped[0]
        gated[...] = shaped[1] * shaped[2]
        lam_j = lam_in[:, j * LANES:(j + 1) * LANES]
        w_j = w_in[:, j * LANES:(j + 1) * LANES]
        gain = jnp.broadcast_to(skip_in[:, cols], (CHUNKS, LANES))
        chunk = iota((CHUNKS, LANES), 0)

        def lines(table):
            return [jnp.broadcast_to(table[m:m + 1], (CHUNKS, LANES)) for m in range(modes)]

        def total(values):
            while len(values) > 1:
                values = [a + b for a, b in zip(values[::2], values[1::2])]
            return values[0]

        fade = lines(jnp.exp(-lam_j))
        weight = lines(w_j)

        def inside(r, states):
            at = pl.ds(r, CHUNKS, stride=length)
            now = gated[at, :]
            states = [fade[m] * states[m] + weight[m] * now for m in range(modes)]
            mixed[j, at, :] = gain * now + total(states)
            return tuple(states)

        states = lax.fori_loop(
            0, length, inside, tuple(jnp.zeros((CHUNKS, LANES), F32) for _ in range(modes)), unroll=4
        )

        shift = 1
        while shift < CHUNKS:
            over = lines(jnp.exp(-float(length * shift) * lam_j))
            states = [
                states[m] + jnp.where(chunk >= shift, over[m] * pltpu.roll(states[m], shift, 0), 0.0)
                for m in range(modes)
            ]
            shift *= 2
        states = tuple(fade[m] * jnp.where(chunk >= 1, pltpu.roll(states[m], 1, 0), 0.0) for m in range(modes))

        def across(r, states):
            at = pl.ds(r, CHUNKS, stride=length)
            mixed[j, at, :] = mixed[j, at, :] + total(list(states))
            return tuple(fade[m] * states[m] for m in range(modes))

        lax.fori_loop(0, length, across, states, unroll=4)

    for j in range(tiles // 2):
        local_tile(j)

    fade_z = jnp.exp(-(span * NX) * lam)
    for o in range(nz - 1, 0, -1):
        @pl.when(z >= o)
        def _(o=o):
            p2_copy(o).wait_recv()
            acc[...] = fade_z * acc[...] + p2[o]

    carry = acc[...]
    p3_copies = []
    for member in range(NX):
        hsend[member] = carry + pre[member]
        carry = fade_row * carry
        p3_copies.append(
            send(hsend.at[member], p3.at[x], p3_send.at[member], p3_recv.at[x], sec_next, z * NX + member)
        )
        p3_copies[-1].start()

    for j in range(tiles // 2, tiles):
        local_tile(j)

    for j in range(tiles):
        send(hsend.at[0], p3.at[j], p3_send.at[0], p3_recv.at[j], sec_next, ctx).wait_recv()
    for j in range(tiles):
        cols = pl.ds(j * LANES, LANES)
        state = p3[j]
        spread = jnp.where(keep, jnp.concatenate([state] * (block // modes), axis=0), 0.0)
        wide = pl.ds(j * block, block)
        carried = dot3((out_hi[:, wide], out_lo[:, wide]), split(spread))
        out_ref[0, :, cols] = (query[:, cols] * (mixed[j] + carried)).astype(BF16)

    for copy in ship + [halo_copy] + feat_copies + p1_copies + p3_copies:
        copy.wait_send()

    @pl.when(jnp.logical_and(x == NX - 1, z < nz - 1))
    def _():
        for q in range(NX):
            edge_copy(q).wait_send()

    for o in range(1, nz):
        @pl.when(z + o < nz)
        def _(o=o):
            p2_copy(o).wait_send()


def on_device(n_section, n_ctx, features, conv_weight, residues, decay_rates, skip_gain):
    _, rows, width = features.shape
    channels = skip_gain.shape[1]
    _, groups, modes = residues.shape
    tiles = channels // LANES
    nz = n_ctx // NX
    vmem = pltpu.VMEM
    dma = pltpu.SemaphoreType.DMA
    whole = pl.BlockSpec(memory_space=pltpu.VMEM)
    conv_weight = jnp.swapaxes(conv_weight, 0, 1)
    residues = jnp.swapaxes(residues, 1, 2)
    decay_rates = jnp.swapaxes(decay_rates, 1, 2)
    return pl.pallas_call(
        functools.partial(kernel, n_section, n_ctx, rows, channels, groups, modes),
        out_shape=pltpu.VMEM((1, rows, channels), BF16),
        in_specs=[pl.BlockSpec(memory_space=pl.ANY)] + [whole] * 4,
        out_specs=whole,
        scratch_shapes=[
            vmem((rows, 2 * channels), BF16),
            vmem((16, channels), BF16),
            vmem((tiles, modes, LANES), F32),
            vmem((tiles, modes, LANES), F32),
            vmem((rows, LANES), BF16),
            vmem((rows, LANES), BF16),
            vmem((tiles, modes + 8, LANES), F32),
            vmem((2, width), F32),
            vmem((NX, modes + 8, LANES), F32),
            vmem((8, LANES), F32),
            vmem((modes, LANES), F32),
            vmem((nz, modes, LANES), F32),
            vmem((modes, LANES), F32),
            vmem((NX, modes, LANES), F32),
            vmem((NX, modes, LANES), F32),
            vmem((tiles, modes, LANES), F32),
            vmem((tiles, 3, rows, LANES), BF16),
            vmem((2, width), F32),
            vmem(conv_weight.shape, F32),
            vmem(residues.shape, F32),
            vmem(decay_rates.shape, F32),
            vmem(skip_gain.shape, F32),
            vmem((rows, LANES), F32),
            vmem((rows, channels), F32),
            vmem((tiles, rows, LANES), F32),
            vmem((rows, groups * modes), BF16),
            vmem((rows, groups * modes), BF16),
            dma((2,)),
            dma((4,)), dma((4,)),
            dma((tiles, 3)), dma((tiles, 3)),
            dma((1,)), dma((1,)),
            dma((NX,)), dma((NX,)),
            dma((NX,)), dma((1,)),
            dma((nz,)), dma((nz,)),
            dma((NX,)), dma((NX,)),
        ],
        compiler_params=pltpu.CompilerParams(collective_id=0, has_side_effects=True),
        name="mixer",
    )(features, conv_weight, residues, decay_rates, skip_gain)


def solution(mesh):
    placed = (
        P("section", "ctx", None),
        P("section", None, None),
        P("section", None, None),
        P("section", None, None),
        P("section", None),
    )
    body = functools.partial(on_device, mesh.shape["section"], mesh.shape["ctx"])
    return jax.shard_map(body, mesh=mesh, in_specs=placed, out_specs=P("section", "ctx", None), check_vma=False)
```

```python
import functools

import jax
import jax.numpy as jnp
from jax import lax
from jax.experimental import pallas as pl
from jax.experimental.pallas import tpu as pltpu
from jax.sharding import PartitionSpec as P

MESH = pl.DeviceIdType.MESH
HIGHEST = lax.Precision.HIGHEST
F32 = jnp.float32
BF16 = jnp.bfloat16
NX = 4
LANES = 128
CHUNKS = 8


def iota(shape, axis):
    return lax.broadcasted_iota(jnp.int32, shape, axis)


def split(value):
    high = value.astype(BF16)
    return high, (value - high.astype(F32)).astype(BF16)


def dot3(left, right):
    dot = functools.partial(jnp.dot, preferred_element_type=F32)
    return dot(left[0], right[0]) + (dot(left[1], right[0]) + dot(left[0], right[1]))


def mode_scale(residues, decay):
    twice = 2.0 * decay
    series = jnp.full_like(twice, 1.0)
    for order in range(10, 1, -1):
        series = 1.0 - series * twice * (1.0 / order)
    gain = jnp.where(twice < 0.5, twice * series, 1.0 - jnp.exp(-twice))
    return residues * jnp.sqrt(gain)


def over_channels(table, channels):
    groups = table.shape[1]
    pick = (iota((groups, channels), 0) == iota((groups, channels), 1) // (channels // groups)).astype(F32)
    return lax.dot_general(table, pick, (((1,), (0,)), ((), ())), precision=HIGHEST, preferred_element_type=F32)


def flat_row(table):
    modes, groups = table.shape
    size = groups * modes
    pick = (iota((modes, size), 0) == iota((modes, size), 1) % modes).astype(F32)
    spread = lax.dot_general(table, pick, (((0,), (0,)), ((), ())), precision=HIGHEST, preferred_element_type=F32)
    keep = iota((groups, size), 0) == iota((groups, size), 1) // modes
    return jnp.sum(jnp.where(keep, spread, 0.0), axis=0, keepdims=True)


def kernel(
    n_section, n_ctx, rows, channels, groups, modes,
    feat_ref, conv_ref, res_ref, dec_ref, skip_ref, out_ref,
    kv, qlast, own_lam, own_w, gate_hi, gate_lo, outbox, esend, p1, ebox, rsend, p2, acc, pre, hsend, p3,
    fbox, halo, conv_in, res_in, dec_in, skip_in, gated, query, mixed, out_hi, out_lo,
    local_sem, par_send, par_recv, feat_send, feat_recv, halo_send, halo_recv,
    p1_send, p1_recv, edge_send, edge_recv, p2_send, p2_recv, p3_send, p3_recv, here,
):
    nz = n_ctx // NX
    tiles = channels // LANES
    length = rows // CHUNKS
    per = channels // groups
    block = (LANES // per) * modes
    sec = lax.axis_index("section")
    ctx = lax.axis_index("ctx")
    z = ctx // NX
    x = ctx % NX
    sec_next = (sec + 1) % n_section
    sec_prev = (sec + n_section - 1) % n_section

    kv_copy = pltpu.make_async_copy(feat_ref.at[0, :, pl.ds(channels, 2 * channels)], kv, local_sem.at[0])
    kv_copy.start()
    q_copy = pltpu.make_async_copy(feat_ref.at[0, pl.ds(rows - 16, 16), pl.ds(0, channels)], qlast, local_sem.at[1])
    q_copy.start()

    barrier = pltpu.get_barrier_semaphore()

    def greet(section, position):
        pl.semaphore_signal(barrier, inc=1, device_id=(section, position), device_id_type=MESH)

    z_next = (z + 1) % nz
    z_prev = (z + nz - 1) % nz
    for o in range(1, NX):
        greet(sec, z * NX + (x + o) % NX)
    for o in range(NX):
        greet(sec, z_next * NX + o)
        greet(sec, z_prev * NX + o)
        greet(sec_next, z * NX + o)
        greet(sec_prev, z * NX + o)

    @pl.when(x == NX - 1)
    def _():
        greet(sec_next, z_next * NX)

    @pl.when(x == 0)
    def _():
        greet(sec_prev, z_prev * NX + NX - 1)

    n_greet = (NX - 1) + 4 * NX

    decay = dec_ref[0]
    scale = mode_scale(res_ref[0], decay)
    lam_wide = over_channels(decay, channels)
    w_wide = over_channels(scale, channels)
    lam_row = flat_row(decay)
    w_row = flat_row(scale)
    for j in range(tiles):
        own_lam[j] = lam_wide[:, j * LANES:(j + 1) * LANES]
        own_w[j] = w_wide[:, j * LANES:(j + 1) * LANES]

    kv_copy.wait()
    q_copy.wait()
    row = iota((rows, LANES), 0)
    to_end = (rows - 1 - row).astype(F32)
    keep = iota((block, LANES), 0) // modes == iota((block, LANES), 1) // per

    esend[:, pl.ds(0, channels)] = qlast[...].astype(F32)[14:]
    esend[:, pl.ds(channels, 2 * channels)] = kv[pl.ds(rows - 16, 16), :].astype(F32)[14:]

    pl.semaphore_wait(barrier, n_greet + (x == NX - 1).astype(jnp.int32) + (x == 0).astype(jnp.int32))

    def send(source, target, send_sem, recv_sem, section, position):
        return pltpu.make_async_remote_copy(
            src_ref=source, dst_ref=target, send_sem=send_sem, recv_sem=recv_sem,
            device_id=(section, position), device_id_type=MESH,
        )

    def pass_on(n):
        for row_of in (z_next, z_prev):
            pl.semaphore_signal(here.at[n], inc=1, device_id=(sec, row_of * NX + x), device_id_type=MESH)

    rounds = nz // 2 - 1
    pass_on(0)

    ship = []
    for n, (source, target) in enumerate(((conv_ref, conv_in), (res_ref, res_in), (dec_ref, dec_in), (skip_ref, skip_in))):
        ship.append(send(source, target, par_send.at[n], par_recv.at[n], sec_next, ctx))
    feat_copies = []
    for j in range(tiles):
        for part in range(3):
            feat_copies.append(
                send(
                    feat_ref.at[0, :, pl.ds(part * channels + j * LANES, LANES)], fbox.at[j, part],
                    feat_send.at[j, part], feat_recv.at[j, part], sec_next, ctx,
                )
            )
    halo_copy = send(esend, halo, halo_send.at[0], halo_recv.at[0], sec_next, (ctx + 1) % n_ctx)
    for copy in ship + [halo_copy] + feat_copies:
        copy.start()

    for j in range(tiles):
        parts = []
        edges = []
        for part in range(2):
            cols = pl.ds(part * channels + j * LANES, LANES)
            value = kv[:, cols].astype(F32)
            taps = [conv_ref[i, :, pl.ds((part + 1) * channels + j * LANES, LANES)] for i in range(3)]
            parts.append(taps[0] * value + taps[1] * pltpu.roll(value, 1, 0) + taps[2] * pltpu.roll(value, 2, 0))
            edges.append(value)
        gate = split(jnp.where(row >= 2, parts[0] * parts[1], 0.0))
        rising = w_row[:, j * block:(j + 1) * block] * jnp.exp(-lam_row[:, j * block:(j + 1) * block] * to_end)
        state = dot3(split(rising.T), gate)
        state = jnp.where(keep, state, 0.0).reshape(block // modes, modes, LANES).sum(axis=0)
        outbox[j, pl.ds(0, modes)] = state
        outbox[j, pl.ds(modes, 8)] = jnp.concatenate(
            [edges[0][rows - 2:], edges[1][rows - 2:], edges[0][:2], edges[1][:2]], axis=0
        )

    pl.semaphore_wait(here.at[0], 2)
    if rounds > 1:
        pass_on(1)

    p1_copies = []
    for o in range(1, NX):
        q = (x + o) % NX
        p1_copies.append(send(outbox.at[q], p1.at[o], p1_send.at[o], p1_recv.at[o], sec, z * NX + q))
        p1_copies[-1].start()

    def edge_copy(q):
        return send(
            outbox.at[q, pl.ds(modes, 8)], ebox, edge_send.at[q], edge_recv.at[0], sec,
            (z + 1) % nz * NX + q,
        )

    @pl.when(jnp.logical_and(x == NX - 1, z < nz - 1))
    def _():
        for q in range(NX):
            edge_copy(q).start()

    p1[0] = outbox[x]

    @pl.when(z == 0)
    def _():
        ebox[...] = jnp.zeros_like(ebox)

    acc[...] = jnp.zeros_like(acc)
    lam = own_lam[x]
    w_own = own_w[x]
    for n in range(1, rounds):
        pl.semaphore_wait(here.at[n], 2)
        if n + 1 < rounds:
            pass_on(n + 1)
    for copy in p1_copies:
        copy.wait_recv()

    @pl.when(z > 0)
    def _():
        edge_copy(0).wait_recv()

    span = float(rows)
    fade_row = jnp.exp(-span * lam)
    first = w_own * jnp.exp(-(span - 1.0) * lam)
    second = w_own * jnp.exp(-(span - 2.0) * lam)
    taps = [
        [conv_ref[i, :, pl.ds(pl.multiple_of((part + 1) * channels + x * LANES, LANES), LANES)] for i in range(3)]
        for part in range(2)
    ]
    before = ebox[...]
    total = jnp.zeros((modes, LANES), F32)
    for member in range(NX):
        slot = (x + NX - member) % NX
        edge = p1[slot, pl.ds(modes, 8)]
        products = []
        for part in range(2):
            old2 = before[2 * part:2 * part + 1]
            old1 = before[2 * part + 1:2 * part + 2]
            new0 = edge[4 + 2 * part:5 + 2 * part]
            new1 = edge[5 + 2 * part:6 + 2 * part]
            t0, t1, t2 = taps[part]
            products.append((t0 * new0 + t1 * old1 + t2 * old2, t0 * new1 + t1 * new0 + t2 * old1))
        state = p1[slot, pl.ds(0, modes)]
        state = state + first * (products[0][0] * products[1][0]) + second * (products[0][1] * products[1][1])
        pre[member] = total
        total = fade_row * total + state
        before = edge
    rsend[...] = total

    def p2_copy(o):
        return send(rsend, p2.at[o], p2_send.at[o], p2_recv.at[o], sec, (z + o) % nz * NX + x)

    order = sorted(range(1, nz), key=lambda o: (-min(o, nz - o), o))
    for o in order:
        @pl.when(z + o < nz)
        def _(o=o):
            p2_copy(o).start()

    for copy in ship:
        copy.wait_recv()
    halo_copy.wait_recv()

    @pl.when(ctx == 0)
    def _():
        halo[...] = jnp.zeros_like(halo)

    decay_in = dec_in[0]
    scale_in = mode_scale(res_in[0], decay_in)
    lam_in = over_channels(decay_in, channels)
    w_in = over_channels(scale_in, channels)
    row_in = flat_row(decay_in)
    for j in range(tiles):
        falling = jnp.exp(-row_in[:, j * block:(j + 1) * block] * (row + 1).astype(F32))
        high, low = split(falling)
        out_hi[:, pl.ds(j * block, block)] = high
        out_lo[:, pl.ds(j * block, block)] = low

    def local_tile(j):
        cols = pl.ds(j * LANES, LANES)
        for part in range(3):
            feat_copies[3 * j + part].wait_recv()
        shaped = []
        for part in range(3):
            value = fbox[j, part].astype(F32)
            wide = pl.ds(part * channels + j * LANES, LANES)
            edge = halo[:, wide]
            one = jnp.where(row == 0, edge[1:2], pltpu.roll(value, 1, 0))
            two = jnp.where(row == 0, edge[0:1], jnp.where(row == 1, edge[1:2], pltpu.roll(value, 2, 0)))
            t0, t1, t2 = [conv_in[i, :, wide] for i in range(3)]
            shaped.append(t0 * value + t1 * one + t2 * two)
        query[:, cols] = shaped[0]
        gated[...] = shaped[1] * shaped[2]
        lam_j = lam_in[:, j * LANES:(j + 1) * LANES]
        w_j = w_in[:, j * LANES:(j + 1) * LANES]
        gain = jnp.broadcast_to(skip_in[:, cols], (CHUNKS, LANES))
        chunk = iota((CHUNKS, LANES), 0)

        def lines(table):
            return [jnp.broadcast_to(table[m:m + 1], (CHUNKS, LANES)) for m in range(modes)]

        def total(values):
            while len(values) > 1:
                values = [a + b for a, b in zip(values[::2], values[1::2])]
            return values[0]

        fade = lines(jnp.exp(-lam_j))
        weight = lines(w_j)

        def inside(r, states):
            at = pl.ds(r, CHUNKS, stride=length)
            now = gated[at, :]
            states = [fade[m] * states[m] + weight[m] * now for m in range(modes)]
            mixed[j, at, :] = gain * now + total(states)
            return tuple(states)

        states = lax.fori_loop(
            0, length, inside, tuple(jnp.zeros((CHUNKS, LANES), F32) for _ in range(modes)), unroll=4
        )

        shift = 1
        while shift < CHUNKS:
            over = lines(jnp.exp(-float(length * shift) * lam_j))
            states = [
                states[m] + jnp.where(chunk >= shift, over[m] * pltpu.roll(states[m], shift, 0), 0.0)
                for m in range(modes)
            ]
            shift *= 2
        states = tuple(fade[m] * jnp.where(chunk >= 1, pltpu.roll(states[m], 1, 0), 0.0) for m in range(modes))

        def across(r, states):
            at = pl.ds(r, CHUNKS, stride=length)
            mixed[j, at, :] = mixed[j, at, :] + total(list(states))
            return tuple(fade[m] * states[m] for m in range(modes))

        lax.fori_loop(0, length, across, states, unroll=4)

    for j in range(tiles // 2):
        local_tile(j)

    fade_z = jnp.exp(-(span * NX) * lam)
    for o in range(nz - 1, 0, -1):
        @pl.when(z >= o)
        def _(o=o):
            p2_copy(o).wait_recv()
            acc[...] = fade_z * acc[...] + p2[o]

    carry = acc[...]
    p3_copies = []
    for member in range(NX):
        hsend[member] = carry + pre[member]
        carry = fade_row * carry
        p3_copies.append(
            send(hsend.at[member], p3.at[x], p3_send.at[member], p3_recv.at[x], sec_next, z * NX + member)
        )
        p3_copies[-1].start()

    for j in range(tiles // 2, tiles):
        local_tile(j)

    for j in range(tiles):
        send(hsend.at[0], p3.at[j], p3_send.at[0], p3_recv.at[j], sec_next, ctx).wait_recv()
    for j in range(tiles):
        cols = pl.ds(j * LANES, LANES)
        state = p3[j]
        spread = jnp.where(keep, jnp.concatenate([state] * (block // modes), axis=0), 0.0)
        wide = pl.ds(j * block, block)
        carried = dot3((out_hi[:, wide], out_lo[:, wide]), split(spread))
        out_ref[0, :, cols] = (query[:, cols] * (mixed[j] + carried)).astype(BF16)

    for copy in ship + [halo_copy] + feat_copies + p1_copies + p3_copies:
        copy.wait_send()

    @pl.when(jnp.logical_and(x == NX - 1, z < nz - 1))
    def _():
        for q in range(NX):
            edge_copy(q).wait_send()

    for o in range(1, nz):
        @pl.when(z + o < nz)
        def _(o=o):
            p2_copy(o).wait_send()


def on_device(n_section, n_ctx, features, conv_weight, residues, decay_rates, skip_gain):
    _, rows, width = features.shape
    channels = skip_gain.shape[1]
    _, groups, modes = residues.shape
    tiles = channels // LANES
    nz = n_ctx // NX
    vmem = pltpu.VMEM
    dma = pltpu.SemaphoreType.DMA
    whole = pl.BlockSpec(memory_space=pltpu.VMEM)
    conv_weight = jnp.swapaxes(conv_weight, 0, 1)
    residues = jnp.swapaxes(residues, 1, 2)
    decay_rates = jnp.swapaxes(decay_rates, 1, 2)
    return pl.pallas_call(
        functools.partial(kernel, n_section, n_ctx, rows, channels, groups, modes),
        out_shape=pltpu.VMEM((1, rows, channels), BF16),
        in_specs=[pl.BlockSpec(memory_space=pl.ANY)] + [whole] * 4,
        out_specs=whole,
        scratch_shapes=[
            vmem((rows, 2 * channels), BF16),
            vmem((16, channels), BF16),
            vmem((tiles, modes, LANES), F32),
            vmem((tiles, modes, LANES), F32),
            vmem((rows, LANES), BF16),
            vmem((rows, LANES), BF16),
            vmem((tiles, modes + 8, LANES), F32),
            vmem((2, width), F32),
            vmem((NX, modes + 8, LANES), F32),
            vmem((8, LANES), F32),
            vmem((modes, LANES), F32),
            vmem((nz, modes, LANES), F32),
            vmem((modes, LANES), F32),
            vmem((NX, modes, LANES), F32),
            vmem((NX, modes, LANES), F32),
            vmem((tiles, modes, LANES), F32),
            vmem((tiles, 3, rows, LANES), BF16),
            vmem((2, width), F32),
            vmem(conv_weight.shape, F32),
            vmem(residues.shape, F32),
            vmem(decay_rates.shape, F32),
            vmem(skip_gain.shape, F32),
            vmem((rows, LANES), F32),
            vmem((rows, channels), F32),
            vmem((tiles, rows, LANES), F32),
            vmem((rows, groups * modes), BF16),
            vmem((rows, groups * modes), BF16),
            dma((2,)),
            dma((4,)), dma((4,)),
            dma((tiles, 3)), dma((tiles, 3)),
            dma((1,)), dma((1,)),
            dma((NX,)), dma((NX,)),
            dma((NX,)), dma((1,)),
            dma((nz,)), dma((nz,)),
            dma((NX,)), dma((NX,)),
            pltpu.SemaphoreType.REGULAR((nz // 2 - 1,)),
        ],
        compiler_params=pltpu.CompilerParams(collective_id=0, has_side_effects=True),
        name="mixer",
    )(features, conv_weight, residues, decay_rates, skip_gain)


def solution(mesh):
    placed = (
        P("section", "ctx", None),
        P("section", None, None),
        P("section", None, None),
        P("section", None, None),
        P("section", None),
    )
    body = functools.partial(on_device, mesh.shape["section"], mesh.shape["ctx"])
    return jax.shard_map(body, mesh=mesh, in_specs=placed, out_specs=P("section", "ctx", None), check_vma=False)
```

```python
import functools

import jax
import jax.numpy as jnp
from jax import lax
from jax.experimental import pallas as pl
from jax.experimental.pallas import tpu as pltpu
from jax.sharding import PartitionSpec as P

MESH = pl.DeviceIdType.MESH
HIGHEST = lax.Precision.HIGHEST
F32 = jnp.float32
BF16 = jnp.bfloat16
NX = 4
LANES = 128
CHUNKS = 8


def iota(shape, axis):
    return lax.broadcasted_iota(jnp.int32, shape, axis)


def split(value):
    high = value.astype(BF16)
    return high, (value - high.astype(F32)).astype(BF16)


def dot3(left, right):
    dot = functools.partial(jnp.dot, preferred_element_type=F32)
    return dot(left[0], right[0]) + (dot(left[1], right[0]) + dot(left[0], right[1]))


def mode_scale(residues, decay):
    twice = 2.0 * decay
    series = jnp.full_like(twice, 1.0)
    for order in range(10, 1, -1):
        series = 1.0 - series * twice * (1.0 / order)
    gain = jnp.where(twice < 0.5, twice * series, 1.0 - jnp.exp(-twice))
    return residues * jnp.sqrt(gain)


def over_channels(table, channels):
    groups = table.shape[1]
    pick = (iota((groups, channels), 0) == iota((groups, channels), 1) // (channels // groups)).astype(F32)
    return lax.dot_general(table, pick, (((1,), (0,)), ((), ())), precision=HIGHEST, preferred_element_type=F32)


def flat_row(table):
    modes, groups = table.shape
    size = groups * modes
    pick = (iota((modes, size), 0) == iota((modes, size), 1) % modes).astype(F32)
    spread = lax.dot_general(table, pick, (((0,), (0,)), ((), ())), precision=HIGHEST, preferred_element_type=F32)
    keep = iota((groups, size), 0) == iota((groups, size), 1) // modes
    return jnp.sum(jnp.where(keep, spread, 0.0), axis=0, keepdims=True)


def kernel(
    n_section, n_ctx, rows, channels, groups, modes,
    feat_ref, conv_ref, res_ref, dec_ref, skip_ref, out_ref,
    kv, qlast, own_lam, own_w, gate_hi, gate_lo, outbox, esend, p1, ebox, rsend, p2, acc, pre, hsend, p3,
    fbox, halo, conv_in, res_in, dec_in, skip_in, gated, query, mixed, out_hi, out_lo,
    local_sem, par_send, par_recv, feat_send, feat_recv, halo_send, halo_recv,
    p1_send, p1_recv, edge_send, edge_recv, p2_send, p2_recv, p3_send, p3_recv, here,
):
    nz = n_ctx // NX
    tiles = channels // LANES
    length = rows // CHUNKS
    per = channels // groups
    block = (LANES // per) * modes
    sec = lax.axis_index("section")
    ctx = lax.axis_index("ctx")
    z = ctx // NX
    x = ctx % NX
    sec_next = (sec + 1) % n_section
    sec_prev = (sec + n_section - 1) % n_section

    kv_copy = pltpu.make_async_copy(feat_ref.at[0, :, pl.ds(channels, 2 * channels)], kv, local_sem.at[0])
    kv_copy.start()
    q_copy = pltpu.make_async_copy(feat_ref.at[0, pl.ds(rows - 16, 16), pl.ds(0, channels)], qlast, local_sem.at[1])
    q_copy.start()

    barrier = pltpu.get_barrier_semaphore()

    def greet(section, position):
        pl.semaphore_signal(barrier, inc=1, device_id=(section, position), device_id_type=MESH)

    z_next = (z + 1) % nz
    z_prev = (z + nz - 1) % nz
    for o in range(1, NX):
        greet(sec, z * NX + (x + o) % NX)
    for o in range(NX):
        greet(sec, z_next * NX + o)
        greet(sec, z_prev * NX + o)
        greet(sec_next, z * NX + o)
        greet(sec_prev, z * NX + o)

    @pl.when(x == NX - 1)
    def _():
        greet(sec_next, z_next * NX)

    @pl.when(x == 0)
    def _():
        greet(sec_prev, z_prev * NX + NX - 1)

    n_greet = (NX - 1) + 4 * NX

    decay = dec_ref[0]
    scale = mode_scale(res_ref[0], decay)
    lam_wide = over_channels(decay, channels)
    w_wide = over_channels(scale, channels)
    lam_row = flat_row(decay)
    w_row = flat_row(scale)
    for j in range(tiles):
        own_lam[j] = lam_wide[:, j * LANES:(j + 1) * LANES]
        own_w[j] = w_wide[:, j * LANES:(j + 1) * LANES]

    kv_copy.wait()
    q_copy.wait()
    row = iota((rows, LANES), 0)
    to_end = (rows - 1 - row).astype(F32)
    keep = iota((block, LANES), 0) // modes == iota((block, LANES), 1) // per

    esend[:, pl.ds(0, channels)] = qlast[...].astype(F32)[14:]
    esend[:, pl.ds(channels, 2 * channels)] = kv[pl.ds(rows - 16, 16), :].astype(F32)[14:]

    for j in range(tiles):
        parts = []
        edges = []
        for part in range(2):
            cols = pl.ds(part * channels + j * LANES, LANES)
            value = kv[:, cols].astype(F32)
            taps = [conv_ref[i, :, pl.ds((part + 1) * channels + j * LANES, LANES)] for i in range(3)]
            parts.append(taps[0] * value + taps[1] * pltpu.roll(value, 1, 0) + taps[2] * pltpu.roll(value, 2, 0))
            edges.append(value)
        gate = split(jnp.where(row >= 2, parts[0] * parts[1], 0.0))
        rising = w_row[:, j * block:(j + 1) * block] * jnp.exp(-lam_row[:, j * block:(j + 1) * block] * to_end)
        state = dot3(split(rising.T), gate)
        state = jnp.where(keep, state, 0.0).reshape(block // modes, modes, LANES).sum(axis=0)
        outbox[j, pl.ds(0, modes)] = state
        outbox[j, pl.ds(modes, 8)] = jnp.concatenate(
            [edges[0][rows - 2:], edges[1][rows - 2:], edges[0][:2], edges[1][:2]], axis=0
        )

    pl.semaphore_wait(barrier, n_greet + (x == NX - 1).astype(jnp.int32) + (x == 0).astype(jnp.int32))

    def send(source, target, send_sem, recv_sem, section, position):
        return pltpu.make_async_remote_copy(
            src_ref=source, dst_ref=target, send_sem=send_sem, recv_sem=recv_sem,
            device_id=(section, position), device_id_type=MESH,
        )

    def pass_on(n):
        for row_of in (z_next, z_prev):
            pl.semaphore_signal(here.at[n], inc=1, device_id=(sec, row_of * NX + x), device_id_type=MESH)

    rounds = nz // 2 - 1
    pass_on(0)

    p1_copies = []
    for o in range(1, NX):
        q = (x + o) % NX
        p1_copies.append(send(outbox.at[q], p1.at[o], p1_send.at[o], p1_recv.at[o], sec, z * NX + q))
        p1_copies[-1].start()

    def edge_copy(q):
        return send(
            outbox.at[q, pl.ds(modes, 8)], ebox, edge_send.at[q], edge_recv.at[0], sec,
            (z + 1) % nz * NX + q,
        )

    @pl.when(jnp.logical_and(x == NX - 1, z < nz - 1))
    def _():
        for q in range(NX):
            edge_copy(q).start()

    ship = []
    for n, (source, target) in enumerate(((conv_ref, conv_in), (res_ref, res_in), (dec_ref, dec_in), (skip_ref, skip_in))):
        ship.append(send(source, target, par_send.at[n], par_recv.at[n], sec_next, ctx))
    feat_copies = []
    for j in range(tiles):
        for part in range(3):
            feat_copies.append(
                send(
                    feat_ref.at[0, :, pl.ds(part * channels + j * LANES, LANES)], fbox.at[j, part],
                    feat_send.at[j, part], feat_recv.at[j, part], sec_next, ctx,
                )
            )
    halo_copy = send(esend, halo, halo_send.at[0], halo_recv.at[0], sec_next, (ctx + 1) % n_ctx)
    for copy in ship + [halo_copy] + feat_copies:
        copy.start()

    pl.semaphore_wait(here.at[0], 2)
    if rounds > 1:
        pass_on(1)

    p1[0] = outbox[x]

    @pl.when(z == 0)
    def _():
        ebox[...] = jnp.zeros_like(ebox)

    acc[...] = jnp.zeros_like(acc)
    lam = own_lam[x]
    w_own = own_w[x]
    for n in range(1, rounds):
        pl.semaphore_wait(here.at[n], 2)
        if n + 1 < rounds:
            pass_on(n + 1)
    for copy in p1_copies:
        copy.wait_recv()

    @pl.when(z > 0)
    def _():
        edge_copy(0).wait_recv()

    span = float(rows)
    fade_row = jnp.exp(-span * lam)
    first = w_own * jnp.exp(-(span - 1.0) * lam)
    second = w_own * jnp.exp(-(span - 2.0) * lam)
    taps = [
        [conv_ref[i, :, pl.ds(pl.multiple_of((part + 1) * channels + x * LANES, LANES), LANES)] for i in range(3)]
        for part in range(2)
    ]
    before = ebox[...]
    total = jnp.zeros((modes, LANES), F32)
    for member in range(NX):
        slot = (x + NX - member) % NX
        edge = p1[slot, pl.ds(modes, 8)]
        products = []
        for part in range(2):
            old2 = before[2 * part:2 * part + 1]
            old1 = before[2 * part + 1:2 * part + 2]
            new0 = edge[4 + 2 * part:5 + 2 * part]
            new1 = edge[5 + 2 * part:6 + 2 * part]
            t0, t1, t2 = taps[part]
            products.append((t0 * new0 + t1 * old1 + t2 * old2, t0 * new1 + t1 * new0 + t2 * old1))
        state = p1[slot, pl.ds(0, modes)]
        state = state + first * (products[0][0] * products[1][0]) + second * (products[0][1] * products[1][1])
        pre[member] = total
        total = fade_row * total + state
        before = edge
    rsend[...] = total

    def p2_copy(o):
        return send(rsend, p2.at[o], p2_send.at[o], p2_recv.at[o], sec, (z + o) % nz * NX + x)

    order = sorted(range(1, nz), key=lambda o: (-min(o, nz - o), o))
    for o in order:
        @pl.when(z + o < nz)
        def _(o=o):
            p2_copy(o).start()

    for copy in ship:
        copy.wait_recv()
    halo_copy.wait_recv()

    @pl.when(ctx == 0)
    def _():
        halo[...] = jnp.zeros_like(halo)

    decay_in = dec_in[0]
    scale_in = mode_scale(res_in[0], decay_in)
    lam_in = over_channels(decay_in, channels)
    w_in = over_channels(scale_in, channels)
    row_in = flat_row(decay_in)
    for j in range(tiles):
        falling = jnp.exp(-row_in[:, j * block:(j + 1) * block] * (row + 1).astype(F32))
        high, low = split(falling)
        out_hi[:, pl.ds(j * block, block)] = high
        out_lo[:, pl.ds(j * block, block)] = low

    def local_tile(j):
        cols = pl.ds(j * LANES, LANES)
        for part in range(3):
            feat_copies[3 * j + part].wait_recv()
        shaped = []
        for part in range(3):
            value = fbox[j, part].astype(F32)
            wide = pl.ds(part * channels + j * LANES, LANES)
            edge = halo[:, wide]
            one = jnp.where(row == 0, edge[1:2], pltpu.roll(value, 1, 0))
            two = jnp.where(row == 0, edge[0:1], jnp.where(row == 1, edge[1:2], pltpu.roll(value, 2, 0)))
            t0, t1, t2 = [conv_in[i, :, wide] for i in range(3)]
            shaped.append(t0 * value + t1 * one + t2 * two)
        query[:, cols] = shaped[0]
        gated[...] = shaped[1] * shaped[2]
        lam_j = lam_in[:, j * LANES:(j + 1) * LANES]
        w_j = w_in[:, j * LANES:(j + 1) * LANES]
        gain = jnp.broadcast_to(skip_in[:, cols], (CHUNKS, LANES))
        chunk = iota((CHUNKS, LANES), 0)

        def lines(table):
            return [jnp.broadcast_to(table[m:m + 1], (CHUNKS, LANES)) for m in range(modes)]

        def total(values):
            while len(values) > 1:
                values = [a + b for a, b in zip(values[::2], values[1::2])]
            return values[0]

        fade = lines(jnp.exp(-lam_j))
        weight = lines(w_j)

        def inside(r, states):
            at = pl.ds(r, CHUNKS, stride=length)
            now = gated[at, :]
            states = [fade[m] * states[m] + weight[m] * now for m in range(modes)]
            mixed[j, at, :] = gain * now + total(states)
            return tuple(states)

        states = lax.fori_loop(
            0, length, inside, tuple(jnp.zeros((CHUNKS, LANES), F32) for _ in range(modes)), unroll=4
        )

        shift = 1
        while shift < CHUNKS:
            over = lines(jnp.exp(-float(length * shift) * lam_j))
            states = [
                states[m] + jnp.where(chunk >= shift, over[m] * pltpu.roll(states[m], shift, 0), 0.0)
                for m in range(modes)
            ]
            shift *= 2
        states = tuple(fade[m] * jnp.where(chunk >= 1, pltpu.roll(states[m], 1, 0), 0.0) for m in range(modes))

        def across(r, states):
            at = pl.ds(r, CHUNKS, stride=length)
            mixed[j, at, :] = mixed[j, at, :] + total(list(states))
            return tuple(fade[m] * states[m] for m in range(modes))

        lax.fori_loop(0, length, across, states, unroll=4)

    local_tile(0)

    fade_z = jnp.exp(-(span * NX) * lam)
    for o in range(nz - 1, 0, -1):
        @pl.when(z >= o)
        def _(o=o):
            p2_copy(o).wait_recv()
            acc[...] = fade_z * acc[...] + p2[o]

    carry = acc[...]
    p3_copies = []
    for member in range(NX):
        hsend[member] = carry + pre[member]
        carry = fade_row * carry
        p3_copies.append(
            send(hsend.at[member], p3.at[x], p3_send.at[member], p3_recv.at[x], sec_next, z * NX + member)
        )
        p3_copies[-1].start()

    for j in range(1, tiles):
        local_tile(j)

    for j in range(tiles):
        send(hsend.at[0], p3.at[j], p3_send.at[0], p3_recv.at[j], sec_next, ctx).wait_recv()
    for j in range(tiles):
        cols = pl.ds(j * LANES, LANES)
        state = p3[j]
        spread = jnp.where(keep, jnp.concatenate([state] * (block // modes), axis=0), 0.0)
        wide = pl.ds(j * block, block)
        carried = dot3((out_hi[:, wide], out_lo[:, wide]), split(spread))
        out_ref[0, :, cols] = (query[:, cols] * (mixed[j] + carried)).astype(BF16)

    for copy in ship + [halo_copy] + feat_copies + p1_copies + p3_copies:
        copy.wait_send()

    @pl.when(jnp.logical_and(x == NX - 1, z < nz - 1))
    def _():
        for q in range(NX):
            edge_copy(q).wait_send()

    for o in range(1, nz):
        @pl.when(z + o < nz)
        def _(o=o):
            p2_copy(o).wait_send()


def on_device(n_section, n_ctx, features, conv_weight, residues, decay_rates, skip_gain):
    _, rows, width = features.shape
    channels = skip_gain.shape[1]
    _, groups, modes = residues.shape
    tiles = channels // LANES
    nz = n_ctx // NX
    vmem = pltpu.VMEM
    dma = pltpu.SemaphoreType.DMA
    whole = pl.BlockSpec(memory_space=pltpu.VMEM)
    conv_weight = jnp.swapaxes(conv_weight, 0, 1)
    residues = jnp.swapaxes(residues, 1, 2)
    decay_rates = jnp.swapaxes(decay_rates, 1, 2)
    return pl.pallas_call(
        functools.partial(kernel, n_section, n_ctx, rows, channels, groups, modes),
        out_shape=pltpu.VMEM((1, rows, channels), BF16),
        in_specs=[pl.BlockSpec(memory_space=pl.ANY)] + [whole] * 4,
        out_specs=whole,
        scratch_shapes=[
            vmem((rows, 2 * channels), BF16),
            vmem((16, channels), BF16),
            vmem((tiles, modes, LANES), F32),
            vmem((tiles, modes, LANES), F32),
            vmem((rows, LANES), BF16),
            vmem((rows, LANES), BF16),
            vmem((tiles, modes + 8, LANES), F32),
            vmem((2, width), F32),
            vmem((NX, modes + 8, LANES), F32),
            vmem((8, LANES), F32),
            vmem((modes, LANES), F32),
            vmem((nz, modes, LANES), F32),
            vmem((modes, LANES), F32),
            vmem((NX, modes, LANES), F32),
            vmem((NX, modes, LANES), F32),
            vmem((tiles, modes, LANES), F32),
            vmem((tiles, 3, rows, LANES), BF16),
            vmem((2, width), F32),
            vmem(conv_weight.shape, F32),
            vmem(residues.shape, F32),
            vmem(decay_rates.shape, F32),
            vmem(skip_gain.shape, F32),
            vmem((rows, LANES), F32),
            vmem((rows, channels), F32),
            vmem((tiles, rows, LANES), F32),
            vmem((rows, groups * modes), BF16),
            vmem((rows, groups * modes), BF16),
            dma((2,)),
            dma((4,)), dma((4,)),
            dma((tiles, 3)), dma((tiles, 3)),
            dma((1,)), dma((1,)),
            dma((NX,)), dma((NX,)),
            dma((NX,)), dma((1,)),
            dma((nz,)), dma((nz,)),
            dma((NX,)), dma((NX,)),
            pltpu.SemaphoreType.REGULAR((nz // 2 - 1,)),
        ],
        compiler_params=pltpu.CompilerParams(collective_id=0, has_side_effects=True),
        name="mixer",
    )(features, conv_weight, residues, decay_rates, skip_gain)


def solution(mesh):
    placed = (
        P("section", "ctx", None),
        P("section", None, None),
        P("section", None, None),
        P("section", None, None),
        P("section", None),
    )
    body = functools.partial(on_device, mesh.shape["section"], mesh.shape["ctx"])
    return jax.shard_map(body, mesh=mesh, in_specs=placed, out_specs=P("section", "ctx", None), check_vma=False)
```

```python
import functools

import jax
import jax.numpy as jnp
from jax import lax
from jax.experimental import pallas as pl
from jax.experimental.pallas import tpu as pltpu
from jax.sharding import PartitionSpec as P

MESH = pl.DeviceIdType.MESH
HIGHEST = lax.Precision.HIGHEST
F32 = jnp.float32
BF16 = jnp.bfloat16
NX = 4
LANES = 128
CHUNKS = 8


def iota(shape, axis):
    return lax.broadcasted_iota(jnp.int32, shape, axis)


def split(value):
    high = value.astype(BF16)
    return high, (value - high.astype(F32)).astype(BF16)


def dot3(left, right):
    dot = functools.partial(jnp.dot, preferred_element_type=F32)
    return dot(left[0], right[0]) + (dot(left[1], right[0]) + dot(left[0], right[1]))


def mode_scale(residues, decay):
    twice = 2.0 * decay
    series = jnp.full_like(twice, 1.0)
    for order in range(10, 1, -1):
        series = 1.0 - series * twice * (1.0 / order)
    gain = jnp.where(twice < 0.5, twice * series, 1.0 - jnp.exp(-twice))
    return residues * jnp.sqrt(gain)


def over_channels(table, channels):
    groups = table.shape[1]
    pick = (iota((groups, channels), 0) == iota((groups, channels), 1) // (channels // groups)).astype(F32)
    return lax.dot_general(table, pick, (((1,), (0,)), ((), ())), precision=HIGHEST, preferred_element_type=F32)


def flat_row(table):
    modes, groups = table.shape
    size = groups * modes
    pick = (iota((modes, size), 0) == iota((modes, size), 1) % modes).astype(F32)
    spread = lax.dot_general(table, pick, (((0,), (0,)), ((), ())), precision=HIGHEST, preferred_element_type=F32)
    keep = iota((groups, size), 0) == iota((groups, size), 1) // modes
    return jnp.sum(jnp.where(keep, spread, 0.0), axis=0, keepdims=True)


def kernel(
    n_section, n_ctx, rows, channels, groups, modes,
    feat_ref, conv_ref, res_ref, dec_ref, skip_ref, out_ref,
    kv, qlast, own_lam, own_w, gate_hi, gate_lo, outbox, esend, p1, ebox, rsend, p2, acc, pre, hsend, p3,
    fbox, halo, conv_in, res_in, dec_in, skip_in, gated, query, mixed, out_hi, out_lo,
    local_sem, par_send, par_recv, feat_send, feat_recv, halo_send, halo_recv,
    p1_send, p1_recv, edge_send, edge_recv, p2_send, p2_recv, p3_send, p3_recv, here,
):
    nz = n_ctx // NX
    tiles = channels // LANES
    length = rows // CHUNKS
    per = channels // groups
    block = (LANES // per) * modes
    sec = lax.axis_index("section")
    ctx = lax.axis_index("ctx")
    z = ctx // NX
    x = ctx % NX
    sec_next = (sec + 1) % n_section
    sec_prev = (sec + n_section - 1) % n_section

    kv_copy = pltpu.make_async_copy(feat_ref.at[0, :, pl.ds(channels, 2 * channels)], kv, local_sem.at[0])
    kv_copy.start()
    q_copy = pltpu.make_async_copy(feat_ref.at[0, pl.ds(rows - 16, 16), pl.ds(0, channels)], qlast, local_sem.at[1])
    q_copy.start()

    barrier = pltpu.get_barrier_semaphore()

    def greet(section, position):
        pl.semaphore_signal(barrier, inc=1, device_id=(section, position), device_id_type=MESH)

    z_next = (z + 1) % nz
    z_prev = (z + nz - 1) % nz
    for o in range(1, NX):
        greet(sec, z * NX + (x + o) % NX)
    for o in range(NX):
        greet(sec, z_next * NX + o)
        greet(sec, z_prev * NX + o)
        greet(sec_next, z * NX + o)
        greet(sec_prev, z * NX + o)

    @pl.when(x == NX - 1)
    def _():
        greet(sec_next, z_next * NX)

    @pl.when(x == 0)
    def _():
        greet(sec_prev, z_prev * NX + NX - 1)

    n_greet = (NX - 1) + 4 * NX

    decay = dec_ref[0]
    scale = mode_scale(res_ref[0], decay)
    lam_wide = over_channels(decay, channels)
    w_wide = over_channels(scale, channels)
    lam_row = flat_row(decay)
    w_row = flat_row(scale)
    for j in range(tiles):
        own_lam[j] = lam_wide[:, j * LANES:(j + 1) * LANES]
        own_w[j] = w_wide[:, j * LANES:(j + 1) * LANES]

    kv_copy.wait()
    q_copy.wait()
    row = iota((rows, LANES), 0)
    to_end = (rows - 1 - row).astype(F32)
    keep = iota((block, LANES), 0) // modes == iota((block, LANES), 1) // per

    esend[:, pl.ds(0, channels)] = qlast[...].astype(F32)[14:]
    esend[:, pl.ds(channels, 2 * channels)] = kv[pl.ds(rows - 16, 16), :].astype(F32)[14:]

    for j in range(tiles):
        parts = []
        edges = []
        for part in range(2):
            cols = pl.ds(part * channels + j * LANES, LANES)
            value = kv[:, cols].astype(F32)
            taps = [conv_ref[i, :, pl.ds((part + 1) * channels + j * LANES, LANES)] for i in range(3)]
            parts.append(taps[0] * value + taps[1] * pltpu.roll(value, 1, 0) + taps[2] * pltpu.roll(value, 2, 0))
            edges.append(value)
        gate = split(jnp.where(row >= 2, parts[0] * parts[1], 0.0))
        rising = w_row[:, j * block:(j + 1) * block] * jnp.exp(-lam_row[:, j * block:(j + 1) * block] * to_end)
        state = dot3(split(rising.T), gate)
        state = jnp.where(keep, state, 0.0).reshape(block // modes, modes, LANES).sum(axis=0)
        outbox[j, pl.ds(0, modes)] = state
        outbox[j, pl.ds(modes, 8)] = jnp.concatenate(
            [edges[0][rows - 2:], edges[1][rows - 2:], edges[0][:2], edges[1][:2]], axis=0
        )

    pl.semaphore_wait(barrier, n_greet + (x == NX - 1).astype(jnp.int32) + (x == 0).astype(jnp.int32))

    def send(source, target, send_sem, recv_sem, section, position):
        return pltpu.make_async_remote_copy(
            src_ref=source, dst_ref=target, send_sem=send_sem, recv_sem=recv_sem,
            device_id=(section, position), device_id_type=MESH,
        )

    def pass_on(n):
        for row_of in (z_next, z_prev):
            pl.semaphore_signal(here.at[n], inc=1, device_id=(sec, row_of * NX + x), device_id_type=MESH)

    rounds = nz // 2 - 1
    pass_on(0)

    p1_copies = []
    for o in range(1, NX):
        q = (x + o) % NX
        p1_copies.append(send(outbox.at[q], p1.at[o], p1_send.at[o], p1_recv.at[o], sec, z * NX + q))
        p1_copies[-1].start()

    def edge_copy(q):
        return send(
            outbox.at[q, pl.ds(modes, 8)], ebox, edge_send.at[q], edge_recv.at[0], sec,
            (z + 1) % nz * NX + q,
        )

    @pl.when(jnp.logical_and(x == NX - 1, z < nz - 1))
    def _():
        for q in range(NX):
            edge_copy(q).start()

    ship = []
    for n, (source, target) in enumerate(((conv_ref, conv_in), (res_ref, res_in), (dec_ref, dec_in), (skip_ref, skip_in))):
        ship.append(send(source, target, par_send.at[n], par_recv.at[n], sec_next, ctx))
    feat_copies = []
    for j, part in [(j, part) for j in range(tiles) for part in (1, 2)] + [(j, 0) for j in range(tiles)]:
        feat_copies.append(
            send(
                feat_ref.at[0, :, pl.ds(part * channels + j * LANES, LANES)], fbox.at[j, part],
                feat_send.at[j, part], feat_recv.at[j, part], sec_next, ctx,
            )
        )
    halo_copy = send(esend, halo, halo_send.at[0], halo_recv.at[0], sec_next, (ctx + 1) % n_ctx)
    for copy in ship + [halo_copy] + feat_copies:
        copy.start()

    pl.semaphore_wait(here.at[0], 2)
    if rounds > 1:
        pass_on(1)

    p1[0] = outbox[x]

    @pl.when(z == 0)
    def _():
        ebox[...] = jnp.zeros_like(ebox)

    acc[...] = jnp.zeros_like(acc)
    lam = own_lam[x]
    w_own = own_w[x]
    for n in range(1, rounds):
        pl.semaphore_wait(here.at[n], 2)
        if n + 1 < rounds:
            pass_on(n + 1)
    for copy in p1_copies:
        copy.wait_recv()

    @pl.when(z > 0)
    def _():
        edge_copy(0).wait_recv()

    span = float(rows)
    fade_row = jnp.exp(-span * lam)
    first = w_own * jnp.exp(-(span - 1.0) * lam)
    second = w_own * jnp.exp(-(span - 2.0) * lam)
    taps = [
        [conv_ref[i, :, pl.ds(pl.multiple_of((part + 1) * channels + x * LANES, LANES), LANES)] for i in range(3)]
        for part in range(2)
    ]
    before = ebox[...]
    total = jnp.zeros((modes, LANES), F32)
    for member in range(NX):
        slot = (x + NX - member) % NX
        edge = p1[slot, pl.ds(modes, 8)]
        products = []
        for part in range(2):
            old2 = before[2 * part:2 * part + 1]
            old1 = before[2 * part + 1:2 * part + 2]
            new0 = edge[4 + 2 * part:5 + 2 * part]
            new1 = edge[5 + 2 * part:6 + 2 * part]
            t0, t1, t2 = taps[part]
            products.append((t0 * new0 + t1 * old1 + t2 * old2, t0 * new1 + t1 * new0 + t2 * old1))
        state = p1[slot, pl.ds(0, modes)]
        state = state + first * (products[0][0] * products[1][0]) + second * (products[0][1] * products[1][1])
        pre[member] = total
        total = fade_row * total + state
        before = edge
    rsend[...] = total

    def p2_copy(o):
        return send(rsend, p2.at[o], p2_send.at[o], p2_recv.at[o], sec, (z + o) % nz * NX + x)

    order = sorted(range(1, nz), key=lambda o: (-min(o, nz - o), o))
    for o in order:
        @pl.when(z + o < nz)
        def _(o=o):
            p2_copy(o).start()

    for copy in ship:
        copy.wait_recv()
    halo_copy.wait_recv()

    @pl.when(ctx == 0)
    def _():
        halo[...] = jnp.zeros_like(halo)

    decay_in = dec_in[0]
    scale_in = mode_scale(res_in[0], decay_in)
    lam_in = over_channels(decay_in, channels)
    w_in = over_channels(scale_in, channels)
    row_in = flat_row(decay_in)
    for j in range(tiles):
        falling = jnp.exp(-row_in[:, j * block:(j + 1) * block] * (row + 1).astype(F32))
        high, low = split(falling)
        out_hi[:, pl.ds(j * block, block)] = high
        out_lo[:, pl.ds(j * block, block)] = low

    def shaped(j, part):
        value = fbox[j, part].astype(F32)
        wide = pl.ds(part * channels + j * LANES, LANES)
        edge = halo[:, wide]
        one = jnp.where(row == 0, edge[1:2], pltpu.roll(value, 1, 0))
        two = jnp.where(row == 0, edge[0:1], jnp.where(row == 1, edge[1:2], pltpu.roll(value, 2, 0)))
        t0, t1, t2 = [conv_in[i, :, wide] for i in range(3)]
        return t0 * value + t1 * one + t2 * two

    def local_tile(j):
        cols = pl.ds(j * LANES, LANES)
        for copy in feat_copies[2 * j:2 * j + 2]:
            copy.wait_recv()
        gated[...] = shaped(j, 1) * shaped(j, 2)
        lam_j = lam_in[:, j * LANES:(j + 1) * LANES]
        w_j = w_in[:, j * LANES:(j + 1) * LANES]
        gain = jnp.broadcast_to(skip_in[:, cols], (CHUNKS, LANES))
        chunk = iota((CHUNKS, LANES), 0)

        def lines(table):
            return [jnp.broadcast_to(table[m:m + 1], (CHUNKS, LANES)) for m in range(modes)]

        def total(values):
            while len(values) > 1:
                values = [a + b for a, b in zip(values[::2], values[1::2])]
            return values[0]

        fade = lines(jnp.exp(-lam_j))
        weight = lines(w_j)

        def inside(r, states):
            at = pl.ds(r, CHUNKS, stride=length)
            now = gated[at, :]
            states = [fade[m] * states[m] + weight[m] * now for m in range(modes)]
            mixed[j, at, :] = gain * now + total(states)
            return tuple(states)

        states = lax.fori_loop(
            0, length, inside, tuple(jnp.zeros((CHUNKS, LANES), F32) for _ in range(modes)), unroll=4
        )

        shift = 1
        while shift < CHUNKS:
            over = lines(jnp.exp(-float(length * shift) * lam_j))
            states = [
                states[m] + jnp.where(chunk >= shift, over[m] * pltpu.roll(states[m], shift, 0), 0.0)
                for m in range(modes)
            ]
            shift *= 2
        states = tuple(fade[m] * jnp.where(chunk >= 1, pltpu.roll(states[m], 1, 0), 0.0) for m in range(modes))

        def across(r, states):
            at = pl.ds(r, CHUNKS, stride=length)
            mixed[j, at, :] = mixed[j, at, :] + total(list(states))
            return tuple(fade[m] * states[m] for m in range(modes))

        lax.fori_loop(0, length, across, states, unroll=4)

    local_tile(0)

    fade_z = jnp.exp(-(span * NX) * lam)
    for o in range(nz - 1, 0, -1):
        @pl.when(z >= o)
        def _(o=o):
            p2_copy(o).wait_recv()
            acc[...] = fade_z * acc[...] + p2[o]

    carry = acc[...]
    p3_copies = []
    for member in range(NX):
        hsend[member] = carry + pre[member]
        carry = fade_row * carry
        p3_copies.append(
            send(hsend.at[member], p3.at[x], p3_send.at[member], p3_recv.at[x], sec_next, z * NX + member)
        )
        p3_copies[-1].start()

    for j in range(1, tiles):
        local_tile(j)

    for j in range(tiles):
        feat_copies[2 * tiles + j].wait_recv()
        query[:, pl.ds(j * LANES, LANES)] = shaped(j, 0)
    for j in range(tiles):
        send(hsend.at[0], p3.at[j], p3_send.at[0], p3_recv.at[j], sec_next, ctx).wait_recv()
    for j in range(tiles):
        cols = pl.ds(j * LANES, LANES)
        state = p3[j]
        spread = jnp.where(keep, jnp.concatenate([state] * (block // modes), axis=0), 0.0)
        wide = pl.ds(j * block, block)
        carried = dot3((out_hi[:, wide], out_lo[:, wide]), split(spread))
        out_ref[0, :, cols] = (query[:, cols] * (mixed[j] + carried)).astype(BF16)

    for copy in ship + [halo_copy] + feat_copies + p1_copies + p3_copies:
        copy.wait_send()

    @pl.when(jnp.logical_and(x == NX - 1, z < nz - 1))
    def _():
        for q in range(NX):
            edge_copy(q).wait_send()

    for o in range(1, nz):
        @pl.when(z + o < nz)
        def _(o=o):
            p2_copy(o).wait_send()


def on_device(n_section, n_ctx, features, conv_weight, residues, decay_rates, skip_gain):
    _, rows, width = features.shape
    channels = skip_gain.shape[1]
    _, groups, modes = residues.shape
    tiles = channels // LANES
    nz = n_ctx // NX
    vmem = pltpu.VMEM
    dma = pltpu.SemaphoreType.DMA
    whole = pl.BlockSpec(memory_space=pltpu.VMEM)
    conv_weight = jnp.swapaxes(conv_weight, 0, 1)
    residues = jnp.swapaxes(residues, 1, 2)
    decay_rates = jnp.swapaxes(decay_rates, 1, 2)
    return pl.pallas_call(
        functools.partial(kernel, n_section, n_ctx, rows, channels, groups, modes),
        out_shape=pltpu.VMEM((1, rows, channels), BF16),
        in_specs=[pl.BlockSpec(memory_space=pl.ANY)] + [whole] * 4,
        out_specs=whole,
        scratch_shapes=[
            vmem((rows, 2 * channels), BF16),
            vmem((16, channels), BF16),
            vmem((tiles, modes, LANES), F32),
            vmem((tiles, modes, LANES), F32),
            vmem((rows, LANES), BF16),
            vmem((rows, LANES), BF16),
            vmem((tiles, modes + 8, LANES), F32),
            vmem((2, width), F32),
            vmem((NX, modes + 8, LANES), F32),
            vmem((8, LANES), F32),
            vmem((modes, LANES), F32),
            vmem((nz, modes, LANES), F32),
            vmem((modes, LANES), F32),
            vmem((NX, modes, LANES), F32),
            vmem((NX, modes, LANES), F32),
            vmem((tiles, modes, LANES), F32),
            vmem((tiles, 3, rows, LANES), BF16),
            vmem((2, width), F32),
            vmem(conv_weight.shape, F32),
            vmem(residues.shape, F32),
            vmem(decay_rates.shape, F32),
            vmem(skip_gain.shape, F32),
            vmem((rows, LANES), F32),
            vmem((rows, channels), F32),
            vmem((tiles, rows, LANES), F32),
            vmem((rows, groups * modes), BF16),
            vmem((rows, groups * modes), BF16),
            dma((2,)),
            dma((4,)), dma((4,)),
            dma((tiles, 3)), dma((tiles, 3)),
            dma((1,)), dma((1,)),
            dma((NX,)), dma((NX,)),
            dma((NX,)), dma((1,)),
            dma((nz,)), dma((nz,)),
            dma((NX,)), dma((NX,)),
            pltpu.SemaphoreType.REGULAR((nz // 2 - 1,)),
        ],
        compiler_params=pltpu.CompilerParams(collective_id=0, has_side_effects=True),
        name="mixer",
    )(features, conv_weight, residues, decay_rates, skip_gain)


def solution(mesh):
    placed = (
        P("section", "ctx", None),
        P("section", None, None),
        P("section", None, None),
        P("section", None, None),
        P("section", None),
    )
    body = functools.partial(on_device, mesh.shape["section"], mesh.shape["ctx"])
    return jax.shard_map(body, mesh=mesh, in_specs=placed, out_specs=P("section", "ctx", None), check_vma=False)
```

```python
import functools

import jax
import jax.numpy as jnp
from jax import lax
from jax.experimental import pallas as pl
from jax.experimental.pallas import tpu as pltpu
from jax.sharding import PartitionSpec as P

MESH = pl.DeviceIdType.MESH
HIGHEST = lax.Precision.HIGHEST
F32 = jnp.float32
BF16 = jnp.bfloat16
NX = 4
LANES = 128
CHUNKS = 8


def iota(shape, axis):
    return lax.broadcasted_iota(jnp.int32, shape, axis)


def split(value):
    high = value.astype(BF16)
    return high, (value - high.astype(F32)).astype(BF16)


def dot3(left, right):
    dot = functools.partial(jnp.dot, preferred_element_type=F32)
    return dot(left[0], right[0]) + (dot(left[1], right[0]) + dot(left[0], right[1]))


def mode_scale(residues, decay):
    twice = 2.0 * decay
    series = jnp.full_like(twice, 1.0)
    for order in range(10, 1, -1):
        series = 1.0 - series * twice * (1.0 / order)
    gain = jnp.where(twice < 0.5, twice * series, 1.0 - jnp.exp(-twice))
    return residues * jnp.sqrt(gain)


def over_channels(table, channels):
    groups = table.shape[1]
    pick = (iota((groups, channels), 0) == iota((groups, channels), 1) // (channels // groups)).astype(F32)
    return lax.dot_general(table, pick, (((1,), (0,)), ((), ())), precision=HIGHEST, preferred_element_type=F32)


def flat_row(table):
    modes, groups = table.shape
    size = groups * modes
    pick = (iota((modes, size), 0) == iota((modes, size), 1) % modes).astype(F32)
    spread = lax.dot_general(table, pick, (((0,), (0,)), ((), ())), precision=HIGHEST, preferred_element_type=F32)
    keep = iota((groups, size), 0) == iota((groups, size), 1) // modes
    return jnp.sum(jnp.where(keep, spread, 0.0), axis=0, keepdims=True)


def kernel(
    n_section, n_ctx, rows, channels, groups, modes,
    feat_ref, conv_ref, res_ref, dec_ref, skip_ref, out_ref,
    kv, qlast, own_lam, own_w, gate_hi, gate_lo, outbox, esend, p1, ebox, rsend, p2, acc, pre, hsend, p3,
    fbox, halo, conv_in, res_in, dec_in, skip_in, gated, mixed, out_hi, out_lo,
    local_sem, par_send, par_recv, feat_send, feat_recv, halo_send, halo_recv,
    p1_send, p1_recv, edge_send, edge_recv, p2_send, p2_recv, p3_send, p3_recv, here,
):
    nz = n_ctx // NX
    tiles = channels // LANES
    length = rows // CHUNKS
    per = channels // groups
    block = (LANES // per) * modes
    sec = lax.axis_index("section")
    ctx = lax.axis_index("ctx")
    z = ctx // NX
    x = ctx % NX
    sec_next = (sec + 1) % n_section
    sec_prev = (sec + n_section - 1) % n_section

    kv_copy = pltpu.make_async_copy(feat_ref.at[0, :, pl.ds(channels, 2 * channels)], kv, local_sem.at[0])
    kv_copy.start()
    q_copy = pltpu.make_async_copy(feat_ref.at[0, pl.ds(rows - 16, 16), pl.ds(0, channels)], qlast, local_sem.at[1])
    q_copy.start()

    barrier = pltpu.get_barrier_semaphore()

    def greet(section, position):
        pl.semaphore_signal(barrier, inc=1, device_id=(section, position), device_id_type=MESH)

    z_next = (z + 1) % nz
    z_prev = (z + nz - 1) % nz
    for o in range(1, NX):
        greet(sec, z * NX + (x + o) % NX)
    for o in range(NX):
        greet(sec, z_next * NX + o)
        greet(sec, z_prev * NX + o)
        greet(sec_next, z * NX + o)
        greet(sec_prev, z * NX + o)

    @pl.when(x == NX - 1)
    def _():
        greet(sec_next, z_next * NX)

    @pl.when(x == 0)
    def _():
        greet(sec_prev, z_prev * NX + NX - 1)

    n_greet = (NX - 1) + 4 * NX

    decay = dec_ref[0]
    scale = mode_scale(res_ref[0], decay)
    lam_wide = over_channels(decay, channels)
    w_wide = over_channels(scale, channels)
    lam_row = flat_row(decay)
    w_row = flat_row(scale)
    for j in range(tiles):
        own_lam[j] = lam_wide[:, j * LANES:(j + 1) * LANES]
        own_w[j] = w_wide[:, j * LANES:(j + 1) * LANES]

    kv_copy.wait()
    q_copy.wait()
    row = iota((rows, LANES), 0)
    to_end = (rows - 1 - row).astype(F32)
    keep = iota((block, LANES), 0) // modes == iota((block, LANES), 1) // per

    esend[:, pl.ds(0, channels)] = qlast[...].astype(F32)[14:]
    esend[:, pl.ds(channels, 2 * channels)] = kv[pl.ds(rows - 16, 16), :].astype(F32)[14:]

    for j in range(tiles):
        parts = []
        edges = []
        for part in range(2):
            cols = pl.ds(part * channels + j * LANES, LANES)
            value = kv[:, cols].astype(F32)
            taps = [conv_ref[i, :, pl.ds((part + 1) * channels + j * LANES, LANES)] for i in range(3)]
            parts.append(taps[0] * value + taps[1] * pltpu.roll(value, 1, 0) + taps[2] * pltpu.roll(value, 2, 0))
            edges.append(value)
        gate = split(jnp.where(row >= 2, parts[0] * parts[1], 0.0))
        rising = w_row[:, j * block:(j + 1) * block] * jnp.exp(-lam_row[:, j * block:(j + 1) * block] * to_end)
        state = dot3(split(rising.T), gate)
        state = jnp.where(keep, state, 0.0).reshape(block // modes, modes, LANES).sum(axis=0)
        outbox[j, pl.ds(0, modes)] = state
        outbox[j, pl.ds(modes, 8)] = jnp.concatenate(
            [edges[0][rows - 2:], edges[1][rows - 2:], edges[0][:2], edges[1][:2]], axis=0
        )

    pl.semaphore_wait(barrier, n_greet + (x == NX - 1).astype(jnp.int32) + (x == 0).astype(jnp.int32))

    def send(source, target, send_sem, recv_sem, section, position):
        return pltpu.make_async_remote_copy(
            src_ref=source, dst_ref=target, send_sem=send_sem, recv_sem=recv_sem,
            device_id=(section, position), device_id_type=MESH,
        )

    def pass_on(n):
        for row_of in (z_next, z_prev):
            pl.semaphore_signal(here.at[n], inc=1, device_id=(sec, row_of * NX + x), device_id_type=MESH)

    rounds = nz // 2 - 1
    pass_on(0)

    p1_copies = []
    for o in range(1, NX):
        q = (x + o) % NX
        p1_copies.append(send(outbox.at[q], p1.at[o], p1_send.at[o], p1_recv.at[o], sec, z * NX + q))
        p1_copies[-1].start()

    def edge_copy(q):
        return send(
            outbox.at[q, pl.ds(modes, 8)], ebox, edge_send.at[q], edge_recv.at[0], sec,
            (z + 1) % nz * NX + q,
        )

    @pl.when(jnp.logical_and(x == NX - 1, z < nz - 1))
    def _():
        for q in range(NX):
            edge_copy(q).start()

    ship = []
    for n, (source, target) in enumerate(((conv_ref, conv_in), (res_ref, res_in), (dec_ref, dec_in), (skip_ref, skip_in))):
        ship.append(send(source, target, par_send.at[n], par_recv.at[n], sec_next, ctx))
    feat_copies = []
    for j, part in [(j, part) for j in range(tiles) for part in (1, 2)] + [(j, 0) for j in range(tiles)]:
        feat_copies.append(
            send(
                feat_ref.at[0, :, pl.ds(part * channels + j * LANES, LANES)], fbox.at[j, part],
                feat_send.at[j, part], feat_recv.at[j, part], sec_next, ctx,
            )
        )
    halo_copy = send(esend, halo, halo_send.at[0], halo_recv.at[0], sec_next, (ctx + 1) % n_ctx)
    for copy in ship + [halo_copy] + feat_copies:
        copy.start()

    pl.semaphore_wait(here.at[0], 2)
    if rounds > 1:
        pass_on(1)

    p1[0] = outbox[x]

    @pl.when(z == 0)
    def _():
        ebox[...] = jnp.zeros_like(ebox)

    acc[...] = jnp.zeros_like(acc)
    lam = own_lam[x]
    w_own = own_w[x]
    for n in range(1, rounds):
        pl.semaphore_wait(here.at[n], 2)
        if n + 1 < rounds:
            pass_on(n + 1)
    for copy in p1_copies:
        copy.wait_recv()

    @pl.when(z > 0)
    def _():
        edge_copy(0).wait_recv()

    span = float(rows)
    fade_row = jnp.exp(-span * lam)
    first = w_own * jnp.exp(-(span - 1.0) * lam)
    second = w_own * jnp.exp(-(span - 2.0) * lam)
    taps = [
        [conv_ref[i, :, pl.ds(pl.multiple_of((part + 1) * channels + x * LANES, LANES), LANES)] for i in range(3)]
        for part in range(2)
    ]
    before = ebox[...]
    total = jnp.zeros((modes, LANES), F32)
    for member in range(NX):
        slot = (x + NX - member) % NX
        edge = p1[slot, pl.ds(modes, 8)]
        products = []
        for part in range(2):
            old2 = before[2 * part:2 * part + 1]
            old1 = before[2 * part + 1:2 * part + 2]
            new0 = edge[4 + 2 * part:5 + 2 * part]
            new1 = edge[5 + 2 * part:6 + 2 * part]
            t0, t1, t2 = taps[part]
            products.append((t0 * new0 + t1 * old1 + t2 * old2, t0 * new1 + t1 * new0 + t2 * old1))
        state = p1[slot, pl.ds(0, modes)]
        state = state + first * (products[0][0] * products[1][0]) + second * (products[0][1] * products[1][1])
        pre[member] = total
        total = fade_row * total + state
        before = edge
    rsend[...] = total

    def p2_copy(o):
        return send(rsend, p2.at[o], p2_send.at[o], p2_recv.at[o], sec, (z + o) % nz * NX + x)

    order = sorted(range(1, nz), key=lambda o: (-min(o, nz - o), o))
    for o in order:
        @pl.when(z + o < nz)
        def _(o=o):
            p2_copy(o).start()

    for copy in ship:
        copy.wait_recv()
    halo_copy.wait_recv()

    @pl.when(ctx == 0)
    def _():
        halo[...] = jnp.zeros_like(halo)

    decay_in = dec_in[0]
    scale_in = mode_scale(res_in[0], decay_in)
    lam_in = over_channels(decay_in, channels)
    w_in = over_channels(scale_in, channels)
    row_in = flat_row(decay_in)
    for j in range(tiles):
        falling = jnp.exp(-row_in[:, j * block:(j + 1) * block] * (row + 1).astype(F32))
        high, low = split(falling)
        out_hi[:, pl.ds(j * block, block)] = high
        out_lo[:, pl.ds(j * block, block)] = low

    def shaped(j, part):
        value = fbox[j, part].astype(F32)
        wide = pl.ds(part * channels + j * LANES, LANES)
        edge = halo[:, wide]
        one = jnp.where(row == 0, edge[1:2], pltpu.roll(value, 1, 0))
        two = jnp.where(row == 0, edge[0:1], jnp.where(row == 1, edge[1:2], pltpu.roll(value, 2, 0)))
        t0, t1, t2 = [conv_in[i, :, wide] for i in range(3)]
        return t0 * value + t1 * one + t2 * two

    def local_tile(j):
        cols = pl.ds(j * LANES, LANES)
        for copy in feat_copies[2 * j:2 * j + 2]:
            copy.wait_recv()
        gated[...] = shaped(j, 1) * shaped(j, 2)
        lam_j = lam_in[:, j * LANES:(j + 1) * LANES]
        w_j = w_in[:, j * LANES:(j + 1) * LANES]
        gain = jnp.broadcast_to(skip_in[:, cols], (CHUNKS, LANES))
        chunk = iota((CHUNKS, LANES), 0)

        def lines(table):
            return [jnp.broadcast_to(table[m:m + 1], (CHUNKS, LANES)) for m in range(modes)]

        def total(values):
            while len(values) > 1:
                values = [a + b for a, b in zip(values[::2], values[1::2])]
            return values[0]

        fade = lines(jnp.exp(-lam_j))
        weight = lines(w_j)

        def inside(r, states):
            at = pl.ds(r, CHUNKS, stride=length)
            now = gated[at, :]
            states = [fade[m] * states[m] + weight[m] * now for m in range(modes)]
            mixed[j, at, :] = gain * now + total(states)
            return tuple(states)

        states = lax.fori_loop(
            0, length, inside, tuple(jnp.zeros((CHUNKS, LANES), F32) for _ in range(modes)), unroll=4
        )

        shift = 1
        while shift < CHUNKS:
            over = lines(jnp.exp(-float(length * shift) * lam_j))
            states = [
                states[m] + jnp.where(chunk >= shift, over[m] * pltpu.roll(states[m], shift, 0), 0.0)
                for m in range(modes)
            ]
            shift *= 2
        states = tuple(fade[m] * jnp.where(chunk >= 1, pltpu.roll(states[m], 1, 0), 0.0) for m in range(modes))

        def across(r, states):
            at = pl.ds(r, CHUNKS, stride=length)
            mixed[j, at, :] = mixed[j, at, :] + total(list(states))
            return tuple(fade[m] * states[m] for m in range(modes))

        lax.fori_loop(0, length, across, states, unroll=4)

    local_tile(0)

    fade_z = jnp.exp(-(span * NX) * lam)
    for o in range(nz - 1, 0, -1):
        @pl.when(z >= o)
        def _(o=o):
            p2_copy(o).wait_recv()
            acc[...] = fade_z * acc[...] + p2[o]

    carry = acc[...]
    p3_copies = []
    for member in range(NX):
        hsend[member] = carry + pre[member]
        carry = fade_row * carry
        p3_copies.append(
            send(hsend.at[member], p3.at[x], p3_send.at[member], p3_recv.at[x], sec_next, z * NX + member)
        )
        p3_copies[-1].start()

    for j in range(1, tiles):
        local_tile(j)

    for j in range(tiles):
        send(hsend.at[0], p3.at[j], p3_send.at[0], p3_recv.at[j], sec_next, ctx).wait_recv()
    for j in range(tiles):
        state = p3[j]
        spread = jnp.where(keep, jnp.concatenate([state] * (block // modes), axis=0), 0.0)
        wide = pl.ds(j * block, block)
        carried = dot3((out_hi[:, wide], out_lo[:, wide]), split(spread))
        mixed[j] = mixed[j] + carried
    for j in range(tiles):
        feat_copies[2 * tiles + j].wait_recv()
        out_ref[0, :, pl.ds(j * LANES, LANES)] = (shaped(j, 0) * mixed[j]).astype(BF16)

    for copy in ship + [halo_copy] + feat_copies + p1_copies + p3_copies:
        copy.wait_send()

    @pl.when(jnp.logical_and(x == NX - 1, z < nz - 1))
    def _():
        for q in range(NX):
            edge_copy(q).wait_send()

    for o in range(1, nz):
        @pl.when(z + o < nz)
        def _(o=o):
            p2_copy(o).wait_send()


def on_device(n_section, n_ctx, features, conv_weight, residues, decay_rates, skip_gain):
    _, rows, width = features.shape
    channels = skip_gain.shape[1]
    _, groups, modes = residues.shape
    tiles = channels // LANES
    nz = n_ctx // NX
    vmem = pltpu.VMEM
    dma = pltpu.SemaphoreType.DMA
    whole = pl.BlockSpec(memory_space=pltpu.VMEM)
    conv_weight = jnp.swapaxes(conv_weight, 0, 1)
    residues = jnp.swapaxes(residues, 1, 2)
    decay_rates = jnp.swapaxes(decay_rates, 1, 2)
    return pl.pallas_call(
        functools.partial(kernel, n_section, n_ctx, rows, channels, groups, modes),
        out_shape=pltpu.VMEM((1, rows, channels), BF16),
        in_specs=[pl.BlockSpec(memory_space=pl.ANY)] + [whole] * 4,
        out_specs=whole,
        scratch_shapes=[
            vmem((rows, 2 * channels), BF16),
            vmem((16, channels), BF16),
            vmem((tiles, modes, LANES), F32),
            vmem((tiles, modes, LANES), F32),
            vmem((rows, LANES), BF16),
            vmem((rows, LANES), BF16),
            vmem((tiles, modes + 8, LANES), F32),
            vmem((2, width), F32),
            vmem((NX, modes + 8, LANES), F32),
            vmem((8, LANES), F32),
            vmem((modes, LANES), F32),
            vmem((nz, modes, LANES), F32),
            vmem((modes, LANES), F32),
            vmem((NX, modes, LANES), F32),
            vmem((NX, modes, LANES), F32),
            vmem((tiles, modes, LANES), F32),
            vmem((tiles, 3, rows, LANES), BF16),
            vmem((2, width), F32),
            vmem(conv_weight.shape, F32),
            vmem(residues.shape, F32),
            vmem(decay_rates.shape, F32),
            vmem(skip_gain.shape, F32),
            vmem((rows, LANES), F32),
            vmem((tiles, rows, LANES), F32),
            vmem((rows, groups * modes), BF16),
            vmem((rows, groups * modes), BF16),
            dma((2,)),
            dma((4,)), dma((4,)),
            dma((tiles, 3)), dma((tiles, 3)),
            dma((1,)), dma((1,)),
            dma((NX,)), dma((NX,)),
            dma((NX,)), dma((1,)),
            dma((nz,)), dma((nz,)),
            dma((NX,)), dma((NX,)),
            pltpu.SemaphoreType.REGULAR((nz // 2 - 1,)),
        ],
        compiler_params=pltpu.CompilerParams(collective_id=0, has_side_effects=True),
        name="mixer",
    )(features, conv_weight, residues, decay_rates, skip_gain)


def solution(mesh):
    placed = (
        P("section", "ctx", None),
        P("section", None, None),
        P("section", None, None),
        P("section", None, None),
        P("section", None),
    )
    body = functools.partial(on_device, mesh.shape["section"], mesh.shape["ctx"])
    return jax.shard_map(body, mesh=mesh, in_specs=placed, out_specs=P("section", "ctx", None), check_vma=False)
```
